512 devices in a mesh: layer: 4 (over y), dp: 4 (over x_lo, core), mp: 32 (over z, x_hi).
Axes of the slice: x: 4 (x_hi: 2, x_lo: 2; x = x_hi * 2 + x_lo), y: 4, z: 16, core: 2. Of those that a mesh axis runs over, the one named last changes fastest.
Arguments:
- mlp_in: bfloat16 [4, 128, 2048], P('layer', 'dp', 'mp'), may hold values from -6 to 6
- gate_weight: bfloat16 [4, 2048, 8192], P('layer', None, ('dp', 'mp')), may hold values from -0.125 to 0.125
- up_weight: bfloat16 [4, 2048, 8192], P('layer', None, ('dp', 'mp')), may hold values from -0.125 to 0.125
- down_weight: bfloat16 [4, 8192, 2048], P('layer', ('dp', 'mp')), may hold values from -0.0625 to 0.0625
- enc_weight: bfloat16 [4, 2048, 16384], P('layer', None, ('dp', 'mp')), may hold values from -0.125 to 0.125
- enc_bias: float32 [4, 16384], P('layer', ('dp', 'mp')), may hold values from -3 to 3
- dec_weight: bfloat16 [4, 4, 16384, 2048], P('layer', None, ('dp', 'mp')), may hold values from -0.046875 to 0.046875
Outputs:
- error_nodes: bfloat16 [4, 128, 2048], P('layer', 'dp', 'mp')
- latents: bfloat16 [4, 128, 16384], P('layer', None, ('dp', 'mp'))
The draws below stay inside these ranges and needn't reach their ends.
All inputs are finite; a program needn't handle non-finite values.
Results may differ from the reference program's by a relative error of at most 0.0049.
Values may be sent and summed in bfloat16 or wider, within the bound.
No kernel may reach another device: no remote copies, remote signals or barrier semaphores. Data moves between devices by JAX's collectives and lax.ppermute only.
A program may use at most 64 MiB of HBM per device.

```python
import jax
import jax.numpy as jnp

D = 2048
FF = 8192
LAT = 16384
TOKENS = 128
LAYERS = 4


def level_of(own_key, dims, pieces, smallest, high):
    level, own = 1.0, jax.random.fold_in(own_key, 6)
    for axis_at, parts in pieces:
        draws = jnp.exp(jax.random.uniform(jax.random.fold_in(own, axis_at), (parts,), jnp.float32, smallest / len(pieces), high / len(pieces)))
        level = level * jnp.repeat(draws, dims[axis_at] // parts).reshape([-1 if axis == axis_at else 1 for axis in range(len(dims))])
    return level


def bell_draw(own_key, dims, scale, limit, cuts=(), dtype=jnp.bfloat16):
    result = scale * jax.random.normal(own_key, dims, jnp.float32)
    if cuts:
        result = result * level_of(own_key, dims, cuts, -0.22, 0.18)
    return jnp.clip(result, -limit, limit).astype(dtype)


def setup_inputs(seed: int = 0) -> dict:
    key_list = jax.random.split(jax.random.key(seed), 8)
    return {
        "mlp_in": bell_draw(key_list[0], (LAYERS, TOKENS, D), 1.0, 6.0, ((0, 4), (1, 4), (2, 32))),
        "gate_weight": bell_draw(key_list[1], (LAYERS, D, FF), D ** -0.5, 0.125, ((0, 4), (2, 128))),
        "up_weight": bell_draw(key_list[2], (LAYERS, D, FF), D ** -0.5, 0.125, ((0, 4), (2, 128))),
        "down_weight": bell_draw(key_list[3], (LAYERS, FF, D), FF ** -0.5, 0.0625, ((0, 4), (1, 128))),
        "enc_weight": bell_draw(key_list[4], (LAYERS, D, LAT), D ** -0.5, 0.125, ((0, 4), (2, 128))),
        "enc_bias": bell_draw(key_list[5], (LAYERS, LAT), 0.5, 3.0, ((0, 4), (1, 128)), jnp.float32),
        "dec_weight": bell_draw(key_list[6], (LAYERS, LAYERS, LAT, D), LAT ** -0.5, 0.046875, ((0, 4), (2, 128))),
    }


def reference(mlp_in, gate_weight, up_weight, down_weight, enc_weight, enc_bias, dec_weight):
    hiddens = []
    codes = []
    for target in range(LAYERS):
        inputs = mlp_in[target]
        gate_part = jnp.dot(inputs, gate_weight[target], preferred_element_type=jnp.float32)
        up_part = jnp.dot(inputs, up_weight[target], preferred_element_type=jnp.float32)
        hiddens.append((jax.nn.silu(gate_part) * up_part).astype(jnp.bfloat16))
        pre_act = jnp.dot(inputs, enc_weight[target], preferred_element_type=jnp.float32)
        pre_act = pre_act + enc_bias[target].astype(jnp.float32)[None, :]
        codes.append(jnp.maximum(pre_act, jnp.float32(0.0)).astype(jnp.bfloat16))
    errors = []
    for target in range(LAYERS):
        running = jnp.dot(hiddens[target], down_weight[target], preferred_element_type=jnp.float32)
        for source in range(target + 1):
            running = running - jnp.dot(codes[source], dec_weight[target, source], preferred_element_type=jnp.float32)
        errors.append(running.astype(jnp.bfloat16))
    return jnp.stack(errors), jnp.stack(codes)
```

```python
import jax
import jax.numpy as jnp
from jax import lax
from jax.sharding import Mesh, PartitionSpec as P

DP = ("x_lo", "core")
MP = ("z", "x_hi")


def split_mesh(mesh):
    return Mesh(mesh.devices.reshape(4, 2, 2, 16, 2), ("layer", "x_lo", "core", "z", "x_hi"))


def body(mlp_in, gate_weight, up_weight, down_weight, enc_weight, enc_bias, dec_weight):
    layer_now = lax.axis_index("layer")
    layers = lax.axis_size("layer")
    n_mp = lax.axis_size(MP)
    n_dp = lax.axis_size(DP)
    rows, part = mlp_in.shape[1:]
    width = rows_all = None
    spread = jnp.broadcast_to(mlp_in, (n_mp, rows, part))
    blocks = lax.all_to_all(spread, MP, 0, 0, tiled=True)
    own_rows = blocks.transpose(1, 0, 2).reshape(rows, n_mp * part)
    all_rows = lax.all_gather(own_rows, DP, axis=0, tiled=True)
    tokens, width = all_rows.shape
    gate_part = jnp.dot(all_rows, gate_weight[0], preferred_element_type=jnp.float32)
    up_part = jnp.dot(all_rows, up_weight[0], preferred_element_type=jnp.float32)
    hidden = (jax.nn.silu(gate_part) * up_part).astype(jnp.bfloat16)
    pre_act = (
        jnp.dot(all_rows, enc_weight[0], preferred_element_type=jnp.float32) + enc_bias[0][None, :]
    )
    latent = jnp.maximum(pre_act, jnp.float32(0.0)).astype(jnp.bfloat16)
    every = lax.all_to_all(
        jnp.broadcast_to(latent, (layers,) + latent.shape), "layer", 0, 0, tiled=True
    )
    keep = (lax.iota(jnp.int32, layers) <= layer_now).astype(jnp.bfloat16)
    every = every * keep[:, None, None]
    cat = every.transpose(1, 0, 2).reshape(tokens, -1)
    partial = jnp.dot(hidden, down_weight[0], preferred_element_type=jnp.float32)
    partial = partial - jnp.dot(
        cat, dec_weight[0].reshape(-1, width), preferred_element_type=jnp.float32
    )
    got = lax.all_to_all(
        partial.astype(jnp.bfloat16).reshape(n_dp, rows, width), DP, 0, 0, tiled=True
    )
    mine = got.astype(jnp.float32).sum(0)
    send = mine.astype(jnp.bfloat16).reshape(rows, n_mp, part).transpose(1, 0, 2)
    got = lax.all_to_all(send, MP, 0, 0, tiled=True)
    error = got.astype(jnp.float32).sum(0).astype(jnp.bfloat16)
    return error[None], latent[None]


def solution(mesh):
    return jax.shard_map(
        body,
        mesh=split_mesh(mesh),
        in_specs=(
            P("layer", DP, MP),
            P("layer", None, DP + MP),
            P("layer", None, DP + MP),
            P("layer", DP + MP, None),
            P("layer", None, DP + MP),
            P("layer", DP + MP),
            P("layer", None, DP + MP, None),
        ),
        out_specs=(P("layer", DP, MP), P("layer", None, DP + MP)),
        check_vma=False,
    )
```

```python
import jax
import jax.numpy as jnp
from jax import lax
from jax.sharding import Mesh, PartitionSpec as P

DP = ("x_lo", "core")
MP = ("z", "x_hi")
PLANE = ("x_lo", "z", "x_hi")


def split_mesh(mesh):
    return Mesh(mesh.devices.reshape(4, 2, 2, 16, 2), ("layer", "x_lo", "core", "z", "x_hi"))


def swap(value):
    return lax.ppermute(value, "core", [(0, 1), (1, 0)])


def dot(a, b):
    return jnp.dot(a, b, preferred_element_type=jnp.float32)


def body(mlp_in, gate_weight, up_weight, down_weight, enc_weight, enc_bias, dec_weight):
    layer_now = lax.axis_index("layer")
    layers = lax.axis_size("layer")
    n_lo, n_z, n_hi = (lax.axis_size(a) for a in PLANE)
    rows, part = mlp_in.shape[1:]
    weights = (gate_weight[0], up_weight[0], enc_weight[0], enc_bias, down_weight[0], dec_weight[0])
    pairs = (weights, tuple(swap(w) for w in weights))
    spread = jnp.broadcast_to(mlp_in, (n_lo * n_z * n_hi, rows, part))
    blocks = lax.all_to_all(spread, PLANE, 0, 0, tiled=True)
    x = blocks.reshape(n_lo, n_z * n_hi, rows, part).transpose(0, 2, 1, 3)
    x = x.reshape(n_lo * rows, n_z * n_hi * part)
    tokens, width = x.shape
    hidden, latent = [], []
    for gate, up, enc, bias, _, _ in pairs:
        hidden.append((jax.nn.silu(dot(x, gate)) * dot(x, up)).astype(jnp.bfloat16))
        latent.append(jnp.maximum(dot(x, enc) + bias, jnp.float32(0.0)).astype(jnp.bfloat16))
    both = jnp.stack(latent)
    every = lax.all_to_all(
        jnp.broadcast_to(both, (layers,) + both.shape), "layer", 0, 0, tiled=True
    )
    other_rows = swap(latent[1])
    keep = (lax.iota(jnp.int32, layers) <= layer_now).astype(jnp.bfloat16)
    every = every * keep[:, None, None, None]
    partial = dot(hidden[0], pairs[0][4]) + dot(hidden[1], pairs[1][4])
    for c in (0, 1):
        cat = every[:, c].transpose(1, 0, 2).reshape(tokens, -1)
        partial = partial - dot(cat, pairs[c][5].reshape(-1, width))
    send = partial.astype(jnp.bfloat16).reshape(n_lo, rows, n_z * n_hi, part).transpose(0, 2, 1, 3)
    got = lax.all_to_all(send.reshape(-1, rows, part), PLANE, 0, 0, tiled=True)
    error = got.astype(jnp.float32).sum(0).astype(jnp.bfloat16)
    mine = latent[0].reshape(n_lo, 1, rows, -1)
    theirs = other_rows.reshape(n_lo, 1, rows, -1)
    first = lax.axis_index("core") == 0
    latent_out = jnp.concatenate(
        [jnp.where(first, mine, theirs), jnp.where(first, theirs, mine)], axis=1
    ).reshape(1, 2 * tokens, -1)
    return error[None], latent_out


def solution(mesh):
    return jax.shard_map(
        body,
        mesh=split_mesh(mesh),
        in_specs=(
            P("layer", DP, MP),
            P("layer", None, DP + MP),
            P("layer", None, DP + MP),
            P("layer", DP + MP, None),
            P("layer", None, DP + MP),
            P("layer", DP + MP),
            P("layer", None, DP + MP, None),
        ),
        out_specs=(P("layer", DP, MP), P("layer", None, DP + MP)),
        check_vma=False,
    )
```

```python
import functools

import jax
import jax.numpy as jnp
from jax import lax
from jax.experimental import pallas as pl
from jax.experimental.pallas import tpu as pltpu
from jax.sharding import Mesh, PartitionSpec as P

DP = ("x_lo", "core")
MP = ("z", "x_hi")
X = ("x_hi", "x_lo")
F32 = jnp.float32
BF16 = jnp.bfloat16
VMEM_BYTES = 67_000_000
TAIL = 48
VMEM = pl.BlockSpec(memory_space=pltpu.VMEM)
SMEM = pl.BlockSpec(memory_space=pltpu.SMEM)
ANY = pl.BlockSpec(memory_space=pl.ANY)


def split_mesh(mesh):
    return Mesh(mesh.devices.reshape(4, 2, 2, 16, 2), ("layer", "x_lo", "core", "z", "x_hi"))


def call(kernel, outs, specs, scratch, flops, n_bytes, room, out_specs=VMEM):
    return pl.pallas_call(
        kernel,
        out_shape=outs,
        in_specs=specs,
        out_specs=out_specs,
        scratch_shapes=scratch,
        cost_estimate=pl.CostEstimate(flops=flops, bytes_accessed=n_bytes, transcendentals=0),
        compiler_params=pltpu.CompilerParams(vmem_limit_bytes=VMEM_BYTES - room),
    )


def swap(value):
    return lax.ppermute(value, "core", [(0, 1), (1, 0)])


def dot(a, b):
    return lax.dot_general(a, b, (((1,), (0,)), ((), ())), preferred_element_type=F32)


def dot_t(a, b):
    return lax.dot_general(a, b, (((1,), (1,)), ((), ())), preferred_element_type=F32)


def low_half(shape):
    return lax.broadcasted_iota(jnp.int32, shape, 1) < shape[1] // 2


def offsets(n_ff, n_lat, n_src):
    ends = [0]
    for n in (n_ff, n_ff, n_ff, n_src * n_lat, n_lat, TAIL):
        ends.append(ends[-1] + n)
    return ends


def start_all(sems, pairs):
    copies = []
    for i, (source, target) in enumerate(pairs):
        copies.append(pltpu.make_async_copy(source, target, sems.at[i]))
        copies[-1].start()
    return copies


def wait_all(copies):
    for copy in copies:
        copy.wait()


def pack_kernel(at, bias, gate, up, down, dec, enc, out, buf, sems, out_sems):
    lat = enc.shape[1]
    blocks = enc.shape[0] // lat
    pairs = [(gate, buf.at[at[0] : at[1]]), (up, buf.at[at[1] : at[2]]), (down, buf.at[at[2] : at[3]])]
    pairs += [
        (enc.at[j * lat : (j + 1) * lat], buf.at[at[4] : at[5], j * lat : (j + 1) * lat])
        for j in range(blocks)
    ]
    pairs += [
        (dec.at[s], buf.at[at[3] + s * lat : at[3] + (s + 1) * lat]) for s in range(dec.shape[0])
    ]
    copies = start_all(sems, pairs)
    value = jnp.broadcast_to(bias[...], (16, lat))
    first = value.astype(BF16).astype(F32)
    rest = value - first
    second = rest.astype(BF16).astype(F32)
    third = rest - second
    row = lax.broadcasted_iota(jnp.int32, (16, lat), 0)
    terms = jnp.where(row == 0, first, jnp.where(row == 1, second, third))
    buf[at[5] : at[6]] = jnp.zeros((TAIL, buf.shape[1]), BF16)
    buf[at[5] : at[5] + 16, 0:lat] = terms.astype(BF16)
    n = 3 + blocks
    wait_all(copies[:n])
    leaving = start_all(
        out_sems,
        [
            (buf.at[at[0] : at[3]], out.at[at[0] : at[3]]),
            (buf.at[at[4] : at[6]], out.at[at[4] : at[6]]),
        ],
    )
    for s in range(dec.shape[0]):
        copies[n + s].wait()
        part = pl.ds(at[3] + s * lat, lat)
        leaving.append(pltpu.make_async_copy(buf.at[part], out.at[part], out_sems.at[2 + s]))
        leaving[-1].start()
    wait_all(leaving)


def encode_kernel(at, got, bias, enc, other, x, latent, copies, encs, terms, sems):
    _, n_lo, n_z, half, lanes = got.shape
    lat = enc.shape[1]
    pairs = [(enc, encs.at[:, 0:lat]), (other.at[at[5] : at[5] + 16, 0:lat], terms)]
    pairs += [
        (other.at[at[4] : at[5], j * lat : (j + 1) * lat], encs.at[j * lat : (j + 1) * lat, lat : 2 * lat])
        for j in range(enc.shape[0] // lat)
    ]
    loads = start_all(sems, pairs)
    low = low_half((half, lanes))
    for lo in range(n_lo):
        for z in range(n_z):
            a = got[0, lo, z].astype(F32)
            b = got[1, lo, z].astype(F32)
            top = jnp.where(low, a, pltpu.roll(b, lanes // 2, 1))
            bottom = jnp.where(low, pltpu.roll(a, lanes // 2, 1), b)
            row = lo * 2 * half
            x[row : row + half, z * lanes : (z + 1) * lanes] = top.astype(BF16)
            x[row + half : row + 2 * half, z * lanes : (z + 1) * lanes] = bottom.astype(BF16)
    wait_all(loads)
    pre = dot(x[...], encs[...])
    parts = terms[...].astype(F32)
    theirs = parts[0:1] + parts[1:2] + parts[2:3]
    for c, shift in enumerate((bias[...], theirs)):
        value = pre[:, c * lat : (c + 1) * lat] + shift
        value = jnp.maximum(value, F32(0.0)).astype(BF16)
        latent[:, c * lat : (c + 1) * lat] = value
        for s in range(copies.shape[0]):
            copies[s, :, c * lat : (c + 1) * lat] = value


def hidden_kernel(at, layer, x, latent, gate, up, down, dec, other, out, gates, ups, downs, decs, sems):
    n_ff, lat = gate.shape[0], dec.shape[1]
    pairs = []
    for buffer, mine, i in ((gates, gate, 0), (ups, up, 1), (downs, down, 2)):
        pairs.append((mine, buffer.at[0:n_ff]))
        pairs.append((other.at[at[i] : at[i + 1]], buffer.at[n_ff : 2 * n_ff]))
    theirs = pl.multiple_of(at[3] + layer[0] * lat, lat // 2)
    pairs.append((dec.at[layer[0]], decs.at[0:lat]))
    pairs.append((other.at[pl.ds(theirs, lat)], decs.at[lat : 2 * lat]))
    loads = start_all(sems, pairs)
    rows = x[...]
    wait_all(loads[:4])
    gate_part = dot_t(rows, gates[...])
    up_part = dot_t(rows, ups[...])
    hidden = (gate_part / (1.0 + jnp.exp(-gate_part)) * up_part).astype(BF16)
    wait_all(loads[4:])
    tile = 512
    for n in range(0, x.shape[1], tile):
        value = dot(hidden, downs[:, n : n + tile])
        out[:, n : n + tile] = value - dot(latent[...], decs[:, n : n + tile])


def decode_kernel(at, layer, got, partial, dec, other, out, total, decs, sems):
    n_src, _, _ = got.shape
    lat = dec.shape[1]
    _, n_lo, n_z, half, lanes = out.shape

    def loads(back):
        s = layer[0] - back
        theirs = pl.multiple_of(at[3] + s * lat, lat // 2)
        return (
            pltpu.make_async_copy(dec.at[s], decs.at[back - 1, 0:lat], sems.at[2 * back - 2]),
            pltpu.make_async_copy(
                other.at[pl.ds(theirs, lat)], decs.at[back - 1, lat : 2 * lat], sems.at[2 * back - 1]
            ),
        )

    for back in range(1, n_src):

        @pl.when(layer[0] >= back)
        def _():
            for copy in loads(back):
                copy.start()

    total[...] = partial[...]
    tile = 512
    for back in range(1, n_src):

        @pl.when(layer[0] >= back)
        def _():
            wait_all(loads(back))
            rows = got[layer[0] - back]
            for n in range(0, total.shape[1], tile):
                value = dot(rows, decs[back - 1, :, n : n + tile])
                total[:, n : n + tile] = total[:, n : n + tile] - value

    low = low_half((half, lanes))
    for lo in range(n_lo):
        row = lo * 2 * half
        for z in range(n_z):
            top = total[row : row + half, z * lanes : (z + 1) * lanes]
            bottom = total[row + half : row + 2 * half, z * lanes : (z + 1) * lanes]
            out[0, lo, z] = jnp.where(low, top, pltpu.roll(bottom, lanes // 2, 1)).astype(BF16)
            out[1, lo, z] = jnp.where(low, pltpu.roll(top, lanes // 2, 1), bottom).astype(BF16)


def last_kernel(got, out):
    half, lanes = got.shape[1:]
    total = got[0].astype(F32)
    for z in range(1, got.shape[0]):
        total = total + got[z].astype(F32)
    out[0:half] = total[:, 0 : lanes // 2].astype(BF16)
    out[half : 2 * half] = pltpu.roll(total, lanes // 2, 1)[:, 0 : lanes // 2].astype(BF16)


def body(mlp_in, gate_weight, up_weight, down_weight, enc_weight, enc_bias, dec_weight):
    layer = lax.axis_index("layer").astype(jnp.int32).reshape(1)
    layers = lax.axis_size("layer")
    n_z, n_hi, n_lo = lax.axis_size("z"), lax.axis_size("x_hi"), lax.axis_size("x_lo")
    rows, part = mlp_in.shape[1:]
    half, tokens = rows // 2, rows * n_lo
    gate, up, down = gate_weight[0].T, up_weight[0].T, down_weight[0]
    enc, dec = enc_weight[0], dec_weight[0]
    width, lat = enc.shape
    n_ff = gate.shape[0]
    at = offsets(n_ff, lat, layers)
    dma = pltpu.SemaphoreType.DMA
    block = jnp.concatenate([mlp_in[0, :half], mlp_in[0, half:]], axis=1)
    spread = jnp.broadcast_to(block, (n_z, half, 2 * part))
    got = lax.all_to_all(spread, "z", 0, 0, tiled=True)
    packed = call(
        functools.partial(pack_kernel, at),
        jax.ShapeDtypeStruct((at[-1], width), BF16),
        [VMEM] + [ANY] * 5,
        [pltpu.VMEM((at[-1], width), BF16), dma((3 + width // lat + layers,)), dma((2 + layers,))],
        0,
        4 * at[-1] * width,
        0,
        ANY,
    )(enc_bias, gate, up, down, dec, enc)
    other = swap(packed)
    got = lax.all_gather(got, X, axis=0, tiled=False).reshape(n_hi, n_lo, n_z, half, 2 * part)
    x, latent, copies = call(
        functools.partial(encode_kernel, at),
        (
            jax.ShapeDtypeStruct((tokens, width), BF16),
            jax.ShapeDtypeStruct((tokens, 2 * lat), BF16),
            jax.ShapeDtypeStruct((layers, tokens, 2 * lat), BF16),
        ),
        [VMEM, VMEM, ANY, ANY],
        [pltpu.VMEM((width, 2 * lat), BF16), pltpu.VMEM((16, lat), BF16), dma((2 + width // lat,))],
        4 * tokens * width * lat,
        4 * width * lat,
        400_000,
        (VMEM, VMEM, VMEM),
    )(got, enc_bias, enc, other)
    every = lax.all_to_all(copies, "layer", 0, 0, tiled=True)
    partial = call(
        functools.partial(hidden_kernel, at),
        jax.ShapeDtypeStruct((tokens, width), F32),
        [SMEM, VMEM, VMEM] + [ANY] * 5,
        [pltpu.VMEM((2 * n_ff, width), BF16) for _ in range(3)]
        + [pltpu.VMEM((2 * lat, width), BF16), dma((8,))],
        12 * tokens * width * n_ff + 4 * tokens * width * lat,
        12 * n_ff * width + 4 * lat * width,
        200_000,
    )(layer, x, latent, gate, up, down, dec, other)
    send = call(
        functools.partial(decode_kernel, at),
        jax.ShapeDtypeStruct((n_hi, n_lo, n_z, half, 2 * part), BF16),
        [SMEM, VMEM, VMEM, ANY, ANY],
        [
            pltpu.VMEM((tokens, width), F32),
            pltpu.VMEM((layers - 1, 2 * lat, width), BF16),
            dma((2 * (layers - 1),)),
        ],
        12 * tokens * width * lat,
        12 * lat * width,
        800_000,
    )(layer, every, partial, dec, other)
    got = lax.all_to_all(send.reshape(n_hi * n_lo, n_z, half, 2 * part), X, 0, 0, tiled=True)
    send = got.astype(F32).sum(0).astype(BF16)
    got = lax.all_to_all(send, "z", 0, 0, tiled=True)
    error = call(
        last_kernel,
        jax.ShapeDtypeStruct((rows, part), BF16),
        [VMEM],
        [],
        0,
        2 * n_z * rows * part,
        4_000_000,
    )(got)
    mine = latent[:, :lat].reshape(n_lo, 1, rows, lat)
    theirs = swap(latent[:, lat:]).reshape(n_lo, 1, rows, lat)
    first = lax.axis_index("core") == 0
    latent_out = jnp.concatenate(
        [jnp.where(first, mine, theirs), jnp.where(first, theirs, mine)], axis=1
    ).reshape(1, 2 * tokens, lat)
    return error[None], latent_out


def solution(mesh):
    return jax.shard_map(
        body,
        mesh=split_mesh(mesh),
        in_specs=(
            P("layer", DP, MP),
            P("layer", None, DP + MP),
            P("layer", None, DP + MP),
            P("layer", DP + MP, None),
            P("layer", None, DP + MP),
            P("layer", DP + MP),
            P("layer", None, DP + MP, None),
        ),
        out_specs=(P("layer", DP, MP), P("layer", None, DP + MP)),
        check_vma=False,
    )
```

```python
import jax
import jax.numpy as jnp
from jax import lax
from jax.experimental import pallas as pl
from jax.experimental.pallas import tpu as pltpu
from jax.sharding import Mesh, PartitionSpec as P

DP = ("x_lo", "core")
MP = ("z", "x_hi")
X = ("x_hi", "x_lo")
F32 = jnp.float32
BF16 = jnp.bfloat16
VMEM_BYTES = 8 * 2**20
VMEM = pl.BlockSpec(memory_space=pltpu.VMEM)
SMEM = pl.BlockSpec(memory_space=pltpu.SMEM)
ANY = pl.BlockSpec(memory_space=pl.ANY)


def split_mesh(mesh):
    return Mesh(mesh.devices.reshape(4, 2, 2, 16, 2), ("layer", "x_lo", "core", "z", "x_hi"))


def call(kernel, name, outs, specs, scratch, flops, n_bytes, out_specs=VMEM):
    return pl.pallas_call(
        kernel,
        name=name,
        out_shape=outs,
        in_specs=specs,
        out_specs=out_specs,
        scratch_shapes=scratch,
        cost_estimate=pl.CostEstimate(flops=flops, bytes_accessed=n_bytes, transcendentals=0),
        compiler_params=pltpu.CompilerParams(vmem_limit_bytes=VMEM_BYTES),
    )


def far(weight):
    return pltpu.with_memory_space_constraint(weight, pltpu.HBM)


def dot(a, b):
    return lax.dot_general(a, b, (((1,), (0,)), ((), ())), preferred_element_type=F32)


def dot_t(a, b):
    return lax.dot_general(a, b, (((1,), (1,)), ((), ())), preferred_element_type=F32)


def low_half(shape):
    return lax.broadcasted_iota(jnp.int32, shape, 1) < shape[1] // 2


def start_all(sems, pairs):
    copies = []
    for i, (source, target) in enumerate(pairs):
        copies.append(pltpu.make_async_copy(source, target, sems.at[i]))
        copies[-1].start()
    return copies


def wait_all(copies):
    for copy in copies:
        copy.wait()


def encode_kernel(got, bias, enc, x, latent, copies, weight, sems):
    n_core, n_hi, n_lo, n_z, half, lanes = got.shape
    loads = start_all(sems, [(enc, weight)])
    low = low_half((half, lanes))
    for lo in range(n_lo):
        for core in range(n_core):
            row = (lo * n_core + core) * 2 * half
            for z in range(n_z):
                a = got[core, 0, lo, z].astype(F32)
                b = got[core, 1, lo, z].astype(F32)
                top = jnp.where(low, a, pltpu.roll(b, lanes // 2, 1))
                bottom = jnp.where(low, pltpu.roll(a, lanes // 2, 1), b)
                cols = slice(z * lanes, (z + 1) * lanes)
                x[row : row + half, cols] = top.astype(BF16)
                x[row + half : row + 2 * half, cols] = bottom.astype(BF16)
    wait_all(loads)
    pre = dot(x[...], weight[...]) + bias[...]
    value = jnp.maximum(pre, F32(0.0)).astype(BF16)
    latent[...] = value
    for s in range(copies.shape[0]):
        copies[s] = value


def hidden_kernel(layer, x, latent, gate, up, down, dec, out, gates, ups, downs, decs, sems):
    loads = start_all(
        sems, [(gate, gates), (up, ups), (down, downs), (dec.at[layer[0]], decs)]
    )
    rows = x[...]
    wait_all(loads[:2])
    gate_part = dot_t(rows, gates[...])
    up_part = dot_t(rows, ups[...])
    hidden = (gate_part / (1.0 + jnp.exp(-gate_part)) * up_part).astype(BF16)
    wait_all(loads[2:])
    tile = 256
    for n in range(0, x.shape[1], tile):
        value = dot(hidden, downs[:, n : n + tile])
        out[:, n : n + tile] = value - dot(latent[...], decs[:, n : n + tile])


def decode_kernel(place, got, partial, dec, keep, give, total, decs, sems):
    n_src = got.shape[0]
    layer, core = place[0], place[1]

    def load(back):
        return pltpu.make_async_copy(dec.at[layer - back], decs.at[back - 1], sems.at[back - 1])

    for back in range(1, n_src):

        @pl.when(layer >= back)
        def _():
            load(back).start()

    total[...] = partial[...]
    tile = 256
    for back in range(1, n_src):

        @pl.when(layer >= back)
        def _():
            load(back).wait()
            rows = got[layer - back]
            for n in range(0, total.shape[1], tile):
                total[:, n : n + tile] = total[:, n : n + tile] - dot(
                    rows, decs[back - 1, :, n : n + tile]
                )

    rows = keep.shape[0] // 2
    for lo in range(2):
        mine = pl.multiple_of((2 * lo + core) * rows, rows)
        theirs = pl.multiple_of((2 * lo + 1 - core) * rows, rows)
        keep[lo * rows : (lo + 1) * rows] = total[pl.ds(mine, rows)]
        give[lo * rows : (lo + 1) * rows] = total[pl.ds(theirs, rows)].astype(BF16)


def join_kernel(place, keep, got, out):
    n_hi, n_lo, n_z, half, lanes = out.shape
    other = 1 - place[1]
    low = low_half((half, lanes))
    for lo in range(n_lo):
        row = lo * 2 * half
        for z in range(n_z):
            cols = slice(z * lanes, (z + 1) * lanes)
            value = keep[row : row + 2 * half, cols] + got[other, row : row + 2 * half, cols].astype(F32)
            top, bottom = value[:half], value[half:]
            out[0, lo, z] = jnp.where(low, top, pltpu.roll(bottom, lanes // 2, 1)).astype(BF16)
            out[1, lo, z] = jnp.where(low, pltpu.roll(top, lanes // 2, 1), bottom).astype(BF16)


def last_kernel(got, out):
    half, lanes = got.shape[1:]
    total = got[0].astype(F32)
    for z in range(1, got.shape[0]):
        total = total + got[z].astype(F32)
    out[0:half] = total[:, 0 : lanes // 2].astype(BF16)
    out[half : 2 * half] = pltpu.roll(total, lanes // 2, 1)[:, 0 : lanes // 2].astype(BF16)


def body(mlp_in, gate_weight, up_weight, down_weight, enc_weight, enc_bias, dec_weight):
    place = jnp.stack([lax.axis_index("layer"), lax.axis_index("core")]).astype(jnp.int32)
    layers, n_core = lax.axis_size("layer"), lax.axis_size("core")
    n_z, n_hi, n_lo = lax.axis_size("z"), lax.axis_size("x_hi"), lax.axis_size("x_lo")
    rows, part = mlp_in.shape[1:]
    half, tokens = rows // 2, rows * n_lo * n_core
    gate, up, down = far(gate_weight[0].T), far(up_weight[0].T), far(down_weight[0])
    enc, dec = far(enc_weight[0]), far(dec_weight[0])
    width, lat = enc.shape
    n_ff = gate.shape[0]
    dma = pltpu.SemaphoreType.DMA
    with jax.named_scope("gather_z"):
        block = jnp.concatenate([mlp_in[0, :half], mlp_in[0, half:]], axis=1)
        spread = jnp.broadcast_to(block, (n_z, half, 2 * part))
        spread, place = lax.optimization_barrier((spread, place))
        got = lax.all_to_all(spread, "z", 0, 0, tiled=True)
    with jax.named_scope("gather_x"):
        got = lax.all_to_all(jnp.broadcast_to(got, (n_hi * n_lo,) + got.shape), X, 0, 0, tiled=True)
    with jax.named_scope("gather_core"):
        got = lax.all_gather(got, "core", axis=0, tiled=False)
        got = got.reshape(n_core, n_hi, n_lo, n_z, half, 2 * part)
    with jax.named_scope("encode"):
        x, latent, copies = call(
            encode_kernel,
            "encode",
            (
                jax.ShapeDtypeStruct((tokens, width), BF16),
                jax.ShapeDtypeStruct((tokens, lat), BF16),
                jax.ShapeDtypeStruct((layers, tokens, lat), BF16),
            ),
            [VMEM, VMEM, ANY],
            [pltpu.VMEM((width, lat), BF16), dma((1,))],
            2 * tokens * width * lat,
            2 * width * lat,
            (VMEM, VMEM, VMEM),
        )(got, enc_bias, enc)
    with jax.named_scope("exchange"):
        every = lax.all_to_all(copies, "layer", 0, 0, tiled=True)
    with jax.named_scope("hidden"):
        partial = call(
            hidden_kernel,
            "hidden",
            jax.ShapeDtypeStruct((tokens, width), F32),
            [SMEM, VMEM, VMEM] + [ANY] * 4,
            [pltpu.VMEM((n_ff, width), BF16) for _ in range(3)]
            + [pltpu.VMEM((lat, width), BF16), dma((4,))],
            6 * tokens * width * n_ff + 2 * tokens * width * lat,
            6 * n_ff * width + 2 * lat * width,
        )(place, x, latent, gate, up, down, dec)
    with jax.named_scope("decode"):
        half_sum = (tokens // n_core, width)
        keep, give = call(
            decode_kernel,
            "decode",
            (jax.ShapeDtypeStruct(half_sum, F32), jax.ShapeDtypeStruct(half_sum, BF16)),
            [SMEM, VMEM, VMEM, ANY],
            [
                pltpu.VMEM((tokens, width), F32),
                pltpu.VMEM((layers - 1, lat, width), BF16),
                dma((layers - 1,)),
            ],
            6 * tokens * width * lat,
            6 * lat * width,
            (VMEM, VMEM),
        )(place, every, partial, dec)
    with jax.named_scope("reduce_core"):
        got = lax.all_gather(give, "core", axis=0, tiled=False)
        send = call(
            join_kernel,
            "join",
            jax.ShapeDtypeStruct((n_hi, n_lo, n_z, half, 2 * part), BF16),
            [SMEM, VMEM, VMEM],
            [],
            0,
            8 * tokens * width,
        )(place, keep, got)
    with jax.named_scope("reduce_x"):
        got = lax.all_to_all(send.reshape(n_hi * n_lo, n_z, half, 2 * part), X, 0, 0, tiled=True)
        send = got.astype(F32).sum(0).astype(BF16)
    with jax.named_scope("reduce_z"):
        got = lax.all_to_all(send, "z", 0, 0, tiled=True)
    with jax.named_scope("last"):
        error = call(
            last_kernel,
            "last",
            jax.ShapeDtypeStruct((rows, part), BF16),
            [VMEM],
            [],
            0,
            2 * n_z * rows * part,
        )(got)
    return error[None], latent[None]


def solution(mesh):
    return jax.shard_map(
        body,
        mesh=split_mesh(mesh),
        in_specs=(
            P("layer", DP, MP),
            P("layer", None, DP + MP),
            P("layer", None, DP + MP),
            P("layer", DP + MP, None),
            P("layer", None, DP + MP),
            P("layer", DP + MP),
            P("layer", None, DP + MP, None),
        ),
        out_specs=(P("layer", DP, MP), P("layer", None, DP + MP)),
        check_vma=False,
    )
```

```python
import jax
import jax.numpy as jnp
from jax import lax
from jax.experimental import pallas as pl
from jax.experimental.pallas import tpu as pltpu
from jax.sharding import Mesh, PartitionSpec as P

DP = ("x_lo", "core")
MP = ("z", "x_hi")
X = ("x_hi", "x_lo")
F32 = jnp.float32
BF16 = jnp.bfloat16
VMEM_BYTES = 8 * 2**20
VMEM = pl.BlockSpec(memory_space=pltpu.VMEM)
SMEM = pl.BlockSpec(memory_space=pltpu.SMEM)
ANY = pl.BlockSpec(memory_space=pl.ANY)


def split_mesh(mesh):
    return Mesh(mesh.devices.reshape(4, 2, 2, 16, 2), ("layer", "x_lo", "core", "z", "x_hi"))


def call(kernel, name, outs, specs, scratch, flops, n_bytes, out_specs=VMEM):
    return pl.pallas_call(
        kernel,
        name=name,
        out_shape=outs,
        in_specs=specs,
        out_specs=out_specs,
        scratch_shapes=scratch,
        cost_estimate=pl.CostEstimate(flops=flops, bytes_accessed=n_bytes, transcendentals=0),
        compiler_params=pltpu.CompilerParams(vmem_limit_bytes=VMEM_BYTES),
    )


def far(weight):
    return pltpu.with_memory_space_constraint(weight, pltpu.HBM)


def dot(a, b):
    return lax.dot_general(a, b, (((1,), (0,)), ((), ())), preferred_element_type=F32)


def dot_t(a, b):
    return lax.dot_general(a, b, (((1,), (1,)), ((), ())), preferred_element_type=F32)


def low_half(shape):
    return lax.broadcasted_iota(jnp.int32, shape, 1) < shape[1] // 2


def turn(z, n_z):
    return (z + n_z // 2) % n_z


def start_all(sems, pairs):
    copies = []
    for i, (source, target) in enumerate(pairs):
        copies.append(pltpu.make_async_copy(source, target, sems.at[i]))
        copies[-1].start()
    return copies


def wait_all(copies):
    for copy in copies:
        copy.wait()


def front_kernel(
    place, got, enc, bias, gate, up, down, dec, latent, copies, out, x, encs, shift, gates, ups, downs, decs, sems
):
    n_core, n_hi, n_lo, n_z, half, lanes = got.shape
    loads = start_all(
        sems,
        [
            (enc, encs),
            (bias, shift),
            (gate, gates),
            (up, ups),
            (down, downs),
            (dec.at[place[0]], decs),
        ],
    )
    low = low_half((half, lanes))
    for lo in range(n_lo):
        for core in range(n_core):
            row = (lo * n_core + core) * 2 * half
            for z in range(n_z):
                at = turn(z, n_z)
                a = got[core, 0, lo, at].astype(F32)
                b = got[core, 1, lo, at].astype(F32)
                top = jnp.where(low, a, pltpu.roll(b, lanes // 2, 1))
                bottom = jnp.where(low, pltpu.roll(a, lanes // 2, 1), b)
                cols = slice(z * lanes, (z + 1) * lanes)
                x[row : row + half, cols] = top.astype(BF16)
                x[row + half : row + 2 * half, cols] = bottom.astype(BF16)
    rows = x[...]
    wait_all(loads[:2])
    pre = dot(rows, encs[...]) + shift[...]
    value = jnp.maximum(pre, F32(0.0)).astype(BF16)
    latent[...] = value
    for s in range(copies.shape[0]):
        copies[s] = value
    wait_all(loads[2:4])
    gate_part = dot_t(rows, gates[...])
    up_part = dot_t(rows, ups[...])
    hidden = (gate_part / (1.0 + jnp.exp(-gate_part)) * up_part).astype(BF16)
    wait_all(loads[4:])
    tile = 256
    for n in range(0, x.shape[1], tile):
        cols = slice(n, n + tile)
        out[:, cols] = dot(hidden, downs[:, cols]) - dot(value, decs[:, cols])


def decode_kernel(place, got, partial, dec, keep, give, total, decs, sems):
    n_src = got.shape[0]
    layer, core = place[0], place[1]

    def load(back):
        return pltpu.make_async_copy(dec.at[layer - back], decs.at[back - 1], sems.at[back - 1])

    for back in range(1, n_src):

        @pl.when(layer >= back)
        def _():
            load(back).start()

    total[...] = partial[...]
    tile = 256
    for back in range(1, n_src):

        @pl.when(layer >= back)
        def _():
            load(back).wait()
            rows = got[layer - back]
            for n in range(0, total.shape[1], tile):
                total[:, n : n + tile] = total[:, n : n + tile] - dot(
                    rows, decs[back - 1, :, n : n + tile]
                )

    rows = keep.shape[0] // 2
    for lo in range(2):
        mine = pl.multiple_of((2 * lo + core) * rows, rows)
        theirs = pl.multiple_of((2 * lo + 1 - core) * rows, rows)
        keep[lo * rows : (lo + 1) * rows] = total[pl.ds(mine, rows)]
        give[lo * rows : (lo + 1) * rows] = total[pl.ds(theirs, rows)].astype(BF16)


def join_kernel(place, keep, got, out):
    n_hi, n_lo, n_z, half, lanes = out.shape
    other = 1 - place[1]
    low = low_half((half, lanes))
    for lo in range(n_lo):
        row = lo * 2 * half
        for z in range(n_z):
            cols = slice(z * lanes, (z + 1) * lanes)
            value = keep[row : row + 2 * half, cols] + got[other, row : row + 2 * half, cols].astype(F32)
            top, bottom = value[:half], value[half:]
            at = turn(z, n_z)
            out[0, lo, at] = jnp.where(low, top, pltpu.roll(bottom, lanes // 2, 1)).astype(BF16)
            out[1, lo, at] = jnp.where(low, pltpu.roll(top, lanes // 2, 1), bottom).astype(BF16)


def last_kernel(got, out):
    half, lanes = got.shape[1:]
    total = got[0].astype(F32)
    for z in range(1, got.shape[0]):
        total = total + got[z].astype(F32)
    out[0:half] = total[:, 0 : lanes // 2].astype(BF16)
    out[half : 2 * half] = pltpu.roll(total, lanes // 2, 1)[:, 0 : lanes // 2].astype(BF16)


def body(mlp_in, gate_weight, up_weight, down_weight, enc_weight, enc_bias, dec_weight):
    place = jnp.stack([lax.axis_index("layer"), lax.axis_index("core")]).astype(jnp.int32)
    layers, n_core = lax.axis_size("layer"), lax.axis_size("core")
    n_z, n_hi, n_lo = lax.axis_size("z"), lax.axis_size("x_hi"), lax.axis_size("x_lo")
    rows, part = mlp_in.shape[1:]
    half, tokens = rows // 2, rows * n_lo * n_core
    gate, up, down = far(gate_weight[0].T), far(up_weight[0].T), far(down_weight[0])
    enc, dec = far(enc_weight[0]), far(dec_weight[0])
    width, lat = enc.shape
    n_ff = gate.shape[0]
    dma = pltpu.SemaphoreType.DMA
    with jax.named_scope("gather_z"):
        block = jnp.concatenate([mlp_in[0, :half], mlp_in[0, half:]], axis=1)
        spread = jnp.broadcast_to(block, (n_z, half, 2 * part))
        spread, place = lax.optimization_barrier((spread, place))
        turned = [[turn(z, n_z) for z in range(n_z)]]
        got = lax.all_to_all(spread, "z", 0, 0, axis_index_groups=turned, tiled=True)
    with jax.named_scope("gather_x"):
        got = lax.all_to_all(jnp.broadcast_to(got, (n_hi * n_lo,) + got.shape), X, 0, 0, tiled=True)
    with jax.named_scope("gather_core"):
        got = lax.all_gather(got, "core", axis=0, tiled=False)
        got = got.reshape(n_core, n_hi, n_lo, n_z, half, 2 * part)
    with jax.named_scope("front"):
        latent, copies, partial = call(
            front_kernel,
            "front",
            (
                jax.ShapeDtypeStruct((tokens, lat), BF16),
                jax.ShapeDtypeStruct((layers, tokens, lat), BF16),
                jax.ShapeDtypeStruct((tokens, width), F32),
            ),
            [SMEM, VMEM] + [ANY] * 6,
            [pltpu.VMEM((tokens, width), BF16), pltpu.VMEM((width, lat), BF16), pltpu.VMEM((1, lat), F32)]
            + [pltpu.VMEM((n_ff, width), BF16) for _ in range(3)]
            + [pltpu.VMEM((lat, width), BF16), dma((6,))],
            6 * tokens * width * n_ff + 4 * tokens * width * lat,
            6 * n_ff * width + 4 * lat * width,
            (VMEM, VMEM, VMEM),
        )(place, got, enc, far(enc_bias), gate, up, down, dec)
    with jax.named_scope("exchange"):
        every = lax.all_to_all(copies, "layer", 0, 0, tiled=True)
    with jax.named_scope("decode"):
        half_sum = (tokens // n_core, width)
        keep, give = call(
            decode_kernel,
            "decode",
            (jax.ShapeDtypeStruct(half_sum, F32), jax.ShapeDtypeStruct(half_sum, BF16)),
            [SMEM, VMEM, VMEM, ANY],
            [
                pltpu.VMEM((tokens, width), F32),
                pltpu.VMEM((layers - 1, lat, width), BF16),
                dma((layers - 1,)),
            ],
            6 * tokens * width * lat,
            6 * lat * width,
            (VMEM, VMEM),
        )(place, every, partial, dec)
    with jax.named_scope("reduce_core"):
        got = lax.all_gather(give, "core", axis=0, tiled=False)
        send = call(
            join_kernel,
            "join",
            jax.ShapeDtypeStruct((n_hi, n_lo, n_z, half, 2 * part), BF16),
            [SMEM, VMEM, VMEM],
            [],
            0,
            8 * tokens * width,
        )(place, keep, got)
    with jax.named_scope("reduce_x"):
        got = lax.all_to_all(send.reshape(n_hi * n_lo, n_z, half, 2 * part), X, 0, 0, tiled=True)
        send = got.astype(F32).sum(0).astype(BF16)
    with jax.named_scope("reduce_z"):
        got = lax.all_to_all(send, "z", 0, 0, axis_index_groups=turned, tiled=True)
    with jax.named_scope("last"):
        error = call(
            last_kernel,
            "last",
            jax.ShapeDtypeStruct((rows, part), BF16),
            [VMEM],
            [],
            0,
            2 * n_z * rows * part,
        )(got)
    return error[None], latent[None]


def solution(mesh):
    return jax.shard_map(
        body,
        mesh=split_mesh(mesh),
        in_specs=(
            P("layer", DP, MP),
            P("layer", None, DP + MP),
            P("layer", None, DP + MP),
            P("layer", DP + MP, None),
            P("layer", None, DP + MP),
            P("layer", DP + MP),
            P("layer", None, DP + MP, None),
        ),
        out_specs=(P("layer", DP, MP), P("layer", None, DP + MP)),
        check_vma=False,
    )
```

```python
import jax
import jax.numpy as jnp
from jax import lax
from jax.experimental import pallas as pl
from jax.experimental.pallas import tpu as pltpu
from jax.sharding import Mesh, PartitionSpec as P

DP = ("x_lo", "core")
MP = ("z", "x_hi")
X = ("x_hi", "x_lo")
F32 = jnp.float32
BF16 = jnp.bfloat16
VMEM_BYTES = 8 * 2**20
VMEM = pl.BlockSpec(memory_space=pltpu.VMEM)
SMEM = pl.BlockSpec(memory_space=pltpu.SMEM)
ANY = pl.BlockSpec(memory_space=pl.ANY)


def split_mesh(mesh):
    return Mesh(mesh.devices.reshape(4, 2, 2, 16, 2), ("layer", "x_lo", "core", "z", "x_hi"))


def call(kernel, name, outs, specs, scratch, flops, n_bytes, out_specs=VMEM):
    return pl.pallas_call(
        kernel,
        name=name,
        out_shape=outs,
        in_specs=specs,
        out_specs=out_specs,
        scratch_shapes=scratch,
        cost_estimate=pl.CostEstimate(flops=flops, bytes_accessed=n_bytes, transcendentals=0),
        compiler_params=pltpu.CompilerParams(vmem_limit_bytes=VMEM_BYTES),
    )


def far(weight):
    return pltpu.with_memory_space_constraint(weight, pltpu.HBM)


def dot(a, b):
    return lax.dot_general(a, b, (((1,), (0,)), ((), ())), preferred_element_type=F32)


def dot_t(a, b):
    return lax.dot_general(a, b, (((1,), (1,)), ((), ())), preferred_element_type=F32)


def low_half(shape):
    return lax.broadcasted_iota(jnp.int32, shape, 1) < shape[1] // 2


def turn(z, n_z):
    return (z + n_z // 2) % n_z


def start_all(sems, pairs):
    copies = []
    for i, (source, target) in enumerate(pairs):
        copies.append(pltpu.make_async_copy(source, target, sems.at[i]))
        copies[-1].start()
    return copies


def wait_all(copies):
    for copy in copies:
        copy.wait()


def encode_kernel(got, enc, bias, x, own, copies, encs, shift, sems):
    n_core, n_hi, n_lo, n_z, half, lanes = got.shape
    loads = start_all(sems, [(enc, encs), (bias, shift)])
    low = low_half((half, lanes))
    for lo in range(n_lo):
        for core in range(n_core):
            row = (lo * n_core + core) * 2 * half
            for z in range(n_z):
                at = turn(z, n_z)
                a = got[core, 0, lo, at].astype(F32)
                b = got[core, 1, lo, at].astype(F32)
                top = jnp.where(low, a, pltpu.roll(b, lanes // 2, 1))
                bottom = jnp.where(low, pltpu.roll(a, lanes // 2, 1), b)
                cols = slice(z * lanes, (z + 1) * lanes)
                x[row : row + half, cols] = top.astype(BF16)
                x[row + half : row + 2 * half, cols] = bottom.astype(BF16)
    wait_all(loads)
    pre = dot(x[...], encs[...]) + shift[...]
    value = jnp.maximum(pre, F32(0.0)).astype(BF16)
    own[...] = value
    for s in range(copies.shape[0]):
        copies[s] = value


def hidden_kernel(place, x, own, gate, up, down, dec, out, latent, gates, ups, downs, decs, sems):
    loads = start_all(
        sems, [(gate, gates), (up, ups), (down, downs), (dec.at[place[0]], decs)]
    )
    latent[...] = own[...]
    rows = x[...]
    wait_all(loads[:2])
    gate_part = dot_t(rows, gates[...])
    up_part = dot_t(rows, ups[...])
    hidden = (gate_part / (1.0 + jnp.exp(-gate_part)) * up_part).astype(BF16)
    wait_all(loads[2:])
    tile = 256
    for n in range(0, x.shape[1], tile):
        cols = slice(n, n + tile)
        out[:, cols] = dot(hidden, downs[:, cols]) - dot(own[...], decs[:, cols])


def decode_kernel(place, got, partial, dec, keep, give, total, decs, sems):
    n_src = got.shape[0]
    layer, core = place[0], place[1]

    def load(back):
        return pltpu.make_async_copy(dec.at[layer - back], decs.at[back - 1], sems.at[back - 1])

    for back in range(1, n_src):

        @pl.when(layer >= back)
        def _():
            load(back).start()

    total[...] = partial[...]
    tile = 256
    for back in range(1, n_src):

        @pl.when(layer >= back)
        def _():
            load(back).wait()
            rows = got[layer - back]
            for n in range(0, total.shape[1], tile):
                total[:, n : n + tile] = total[:, n : n + tile] - dot(
                    rows, decs[back - 1, :, n : n + tile]
                )

    rows = keep.shape[0] // 2
    for lo in range(2):
        mine = pl.multiple_of((2 * lo + core) * rows, rows)
        theirs = pl.multiple_of((2 * lo + 1 - core) * rows, rows)
        keep[lo * rows : (lo + 1) * rows] = total[pl.ds(mine, rows)]
        give[lo * rows : (lo + 1) * rows] = total[pl.ds(theirs, rows)].astype(BF16)


def join_kernel(place, keep, got, out):
    n_hi, n_lo, n_z, half, lanes = out.shape
    other = 1 - place[1]
    low = low_half((half, lanes))
    for lo in range(n_lo):
        row = lo * 2 * half
        for z in range(n_z):
            cols = slice(z * lanes, (z + 1) * lanes)
            value = keep[row : row + 2 * half, cols] + got[other, row : row + 2 * half, cols].astype(F32)
            top, bottom = value[:half], value[half:]
            at = turn(z, n_z)
            out[0, lo, at] = jnp.where(low, top, pltpu.roll(bottom, lanes // 2, 1)).astype(BF16)
            out[1, lo, at] = jnp.where(low, pltpu.roll(top, lanes // 2, 1), bottom).astype(BF16)


def last_kernel(got, out):
    half, lanes = got.shape[1:]
    total = got[0].astype(F32)
    for z in range(1, got.shape[0]):
        total = total + got[z].astype(F32)
    out[0:half] = total[:, 0 : lanes // 2].astype(BF16)
    out[half : 2 * half] = pltpu.roll(total, lanes // 2, 1)[:, 0 : lanes // 2].astype(BF16)


def body(mlp_in, gate_weight, up_weight, down_weight, enc_weight, enc_bias, dec_weight):
    place = jnp.stack([lax.axis_index("layer"), lax.axis_index("core")]).astype(jnp.int32)
    layers, n_core = lax.axis_size("layer"), lax.axis_size("core")
    n_z, n_hi, n_lo = lax.axis_size("z"), lax.axis_size("x_hi"), lax.axis_size("x_lo")
    rows, part = mlp_in.shape[1:]
    half, tokens = rows // 2, rows * n_lo * n_core
    gate, up, down = far(gate_weight[0].T), far(up_weight[0].T), far(down_weight[0])
    enc, dec = far(enc_weight[0]), far(dec_weight[0])
    width, lat = enc.shape
    n_ff = gate.shape[0]
    dma = pltpu.SemaphoreType.DMA
    with jax.named_scope("gather_z"):
        block = jnp.concatenate([mlp_in[0, :half], mlp_in[0, half:]], axis=1)
        spread = jnp.broadcast_to(block, (n_z, half, 2 * part))
        spread, place = lax.optimization_barrier((spread, place))
        turned = [[turn(z, n_z) for z in range(n_z)]]
        got = lax.all_to_all(spread, "z", 0, 0, axis_index_groups=turned, tiled=True)
    with jax.named_scope("gather_x"):
        got = lax.all_to_all(jnp.broadcast_to(got, (n_hi * n_lo,) + got.shape), X, 0, 0, tiled=True)
    with jax.named_scope("gather_core"):
        got = lax.all_gather(got, "core", axis=0, tiled=False)
        got = got.reshape(n_core, n_hi, n_lo, n_z, half, 2 * part)
    with jax.named_scope("encode"):
        x, own, copies = call(
            encode_kernel,
            "encode",
            (
                jax.ShapeDtypeStruct((tokens, width), BF16),
                jax.ShapeDtypeStruct((tokens, lat), BF16),
                jax.ShapeDtypeStruct((layers, tokens, lat), BF16),
            ),
            [VMEM, ANY, ANY],
            [pltpu.VMEM((width, lat), BF16), pltpu.VMEM((1, lat), F32), dma((2,))],
            2 * tokens * width * lat,
            2 * width * lat,
            (VMEM, VMEM, VMEM),
        )(got, enc, far(enc_bias))
    with jax.named_scope("exchange"):
        every = lax.all_to_all(copies, "layer", 0, 0, tiled=True)
    with jax.named_scope("hidden"):
        partial, latent = call(
            hidden_kernel,
            "hidden",
            (jax.ShapeDtypeStruct((tokens, width), F32), jax.ShapeDtypeStruct((tokens, lat), BF16)),
            [SMEM, VMEM, VMEM] + [ANY] * 4,
            [pltpu.VMEM((n_ff, width), BF16) for _ in range(3)]
            + [pltpu.VMEM((lat, width), BF16), dma((4,))],
            6 * tokens * width * n_ff + 2 * tokens * width * lat,
            6 * n_ff * width + 2 * lat * width,
            (VMEM, VMEM),
        )(place, x, own, gate, up, down, dec)
    with jax.named_scope("decode"):
        half_sum = (tokens // n_core, width)
        keep, give = call(
            decode_kernel,
            "decode",
            (jax.ShapeDtypeStruct(half_sum, F32), jax.ShapeDtypeStruct(half_sum, BF16)),
            [SMEM, VMEM, VMEM, ANY],
            [
                pltpu.VMEM((tokens, width), F32),
                pltpu.VMEM((layers - 1, lat, width), BF16),
                dma((layers - 1,)),
            ],
            6 * tokens * width * lat,
            6 * lat * width,
            (VMEM, VMEM),
        )(place, every, partial, dec)
    with jax.named_scope("reduce_core"):
        got = lax.all_gather(give, "core", axis=0, tiled=False)
        send = call(
            join_kernel,
            "join",
            jax.ShapeDtypeStruct((n_hi, n_lo, n_z, half, 2 * part), BF16),
            [SMEM, VMEM, VMEM],
            [],
            0,
            8 * tokens * width,
        )(place, keep, got)
    with jax.named_scope("reduce_x"):
        got = lax.all_to_all(send.reshape(n_hi * n_lo, n_z, half, 2 * part), X, 0, 0, tiled=True)
        send = got.astype(F32).sum(0).astype(BF16)
    with jax.named_scope("reduce_z"):
        got = lax.all_to_all(send, "z", 0, 0, axis_index_groups=turned, tiled=True)
    with jax.named_scope("last"):
        error = call(
            last_kernel,
            "last",
            jax.ShapeDtypeStruct((rows, part), BF16),
            [VMEM],
            [],
            0,
            2 * n_z * rows * part,
        )(got)
    return error[None], latent[None]


def solution(mesh):
    return jax.shard_map(
        body,
        mesh=split_mesh(mesh),
        in_specs=(
            P("layer", DP, MP),
            P("layer", None, DP + MP),
            P("layer", None, DP + MP),
            P("layer", DP + MP, None),
            P("layer", None, DP + MP),
            P("layer", DP + MP),
            P("layer", None, DP + MP, None),
        ),
        out_specs=(P("layer", DP, MP), P("layer", None, DP + MP)),
        check_vma=False,
    )
```

```python
import jax
import jax.numpy as jnp
from jax import lax
from jax.experimental import pallas as pl
from jax.experimental.pallas import tpu as pltpu
from jax.sharding import Mesh, PartitionSpec as P

DP = ("x_lo", "core")
MP = ("z", "x_hi")
X = ("x_hi", "x_lo")
F32 = jnp.float32
BF16 = jnp.bfloat16
VMEM_BYTES = 8 * 2**20
VMEM = pl.BlockSpec(memory_space=pltpu.VMEM)
SMEM = pl.BlockSpec(memory_space=pltpu.SMEM)
ANY = pl.BlockSpec(memory_space=pl.ANY)


def split_mesh(mesh):
    return Mesh(mesh.devices.reshape(4, 2, 2, 16, 2), ("layer", "x_lo", "core", "z", "x_hi"))


def call(kernel, name, outs, specs, scratch, flops, n_bytes, out_specs=VMEM):
    return pl.pallas_call(
        kernel,
        name=name,
        out_shape=outs,
        in_specs=specs,
        out_specs=out_specs,
        scratch_shapes=scratch,
        cost_estimate=pl.CostEstimate(flops=flops, bytes_accessed=n_bytes, transcendentals=0),
        compiler_params=pltpu.CompilerParams(vmem_limit_bytes=VMEM_BYTES),
    )


def far(weight):
    return pltpu.with_memory_space_constraint(weight, pltpu.HBM)


def dot(a, b):
    return lax.dot_general(a, b, (((1,), (0,)), ((), ())), preferred_element_type=F32)


def dot_t(a, b):
    return lax.dot_general(a, b, (((1,), (1,)), ((), ())), preferred_element_type=F32)


def low_half(shape):
    return lax.broadcasted_iota(jnp.int32, shape, 1) < shape[1] // 2


def turn(z, n_z):
    return (z + n_z // 2) % n_z


def start_all(sems, pairs):
    copies = []
    for i, (source, target) in enumerate(pairs):
        copies.append(pltpu.make_async_copy(source, target, sems.at[i]))
        copies[-1].start()
    return copies


def wait_all(copies):
    for copy in copies:
        copy.wait()


def encode_kernel(got, enc, bias, x, own, copies, shift, sems):
    n_core, n_hi, n_lo, n_z, half, lanes = got.shape
    loads = start_all(sems, [(bias, shift)])
    low = low_half((half, lanes))
    for lo in range(n_lo):
        for core in range(n_core):
            row = (lo * n_core + core) * 2 * half
            for z in range(n_z):
                at = turn(z, n_z)
                a = got[core, 0, lo, at].astype(F32)
                b = got[core, 1, lo, at].astype(F32)
                top = jnp.where(low, a, pltpu.roll(b, lanes // 2, 1))
                bottom = jnp.where(low, pltpu.roll(a, lanes // 2, 1), b)
                cols = slice(z * lanes, (z + 1) * lanes)
                x[row : row + half, cols] = top.astype(BF16)
                x[row + half : row + 2 * half, cols] = bottom.astype(BF16)
    wait_all(loads)
    pre = dot(x[...], enc[...]) + shift[...]
    value = jnp.maximum(pre, F32(0.0)).astype(BF16)
    own[...] = value
    for s in range(copies.shape[0]):
        copies[s] = value


def hidden_kernel(place, x, own, gate, up, down, dec, out, latent, gates, ups, downs, decs, sems):
    loads = start_all(
        sems, [(gate, gates), (up, ups), (down, downs), (dec.at[place[0]], decs)]
    )
    latent[...] = own[...]
    rows = x[...]
    wait_all(loads[:2])
    gate_part = dot_t(rows, gates[...])
    up_part = dot_t(rows, ups[...])
    hidden = (gate_part / (1.0 + jnp.exp(-gate_part)) * up_part).astype(BF16)
    wait_all(loads[2:])
    tile = 256
    for n in range(0, x.shape[1], tile):
        cols = slice(n, n + tile)
        out[:, cols] = dot(hidden, downs[:, cols]) - dot(own[...], decs[:, cols])


def decode_kernel(place, got, partial, dec, keep, give, total, decs, sems):
    n_src = got.shape[0]
    layer, core = place[0], place[1]

    def load(back):
        return pltpu.make_async_copy(dec.at[layer - back], decs.at[back - 1], sems.at[back - 1])

    for back in range(1, n_src):

        @pl.when(layer >= back)
        def _():
            load(back).start()

    total[...] = partial[...]
    tile = 256
    for back in range(1, n_src):

        @pl.when(layer >= back)
        def _():
            load(back).wait()
            rows = got[layer - back]
            for n in range(0, total.shape[1], tile):
                total[:, n : n + tile] = total[:, n : n + tile] - dot(
                    rows, decs[back - 1, :, n : n + tile]
                )

    rows = keep.shape[0] // 2
    for lo in range(2):
        mine = pl.multiple_of((2 * lo + core) * rows, rows)
        theirs = pl.multiple_of((2 * lo + 1 - core) * rows, rows)
        keep[lo * rows : (lo + 1) * rows] = total[pl.ds(mine, rows)]
        give[lo * rows : (lo + 1) * rows] = total[pl.ds(theirs, rows)].astype(BF16)


def join_kernel(place, keep, got, out):
    n_hi, n_lo, n_z, half, lanes = out.shape
    other = 1 - place[1]
    low = low_half((half, lanes))
    for lo in range(n_lo):
        row = lo * 2 * half
        for z in range(n_z):
            cols = slice(z * lanes, (z + 1) * lanes)
            value = keep[row : row + 2 * half, cols] + got[other, row : row + 2 * half, cols].astype(F32)
            top, bottom = value[:half], value[half:]
            at = turn(z, n_z)
            out[0, lo, at] = jnp.where(low, top, pltpu.roll(bottom, lanes // 2, 1)).astype(BF16)
            out[1, lo, at] = jnp.where(low, pltpu.roll(top, lanes // 2, 1), bottom).astype(BF16)


def last_kernel(got, out):
    half, lanes = got.shape[1:]
    total = got[0].astype(F32)
    for z in range(1, got.shape[0]):
        total = total + got[z].astype(F32)
    out[0:half] = total[:, 0 : lanes // 2].astype(BF16)
    out[half : 2 * half] = pltpu.roll(total, lanes // 2, 1)[:, 0 : lanes // 2].astype(BF16)


def body(mlp_in, gate_weight, up_weight, down_weight, enc_weight, enc_bias, dec_weight):
    place = jnp.stack([lax.axis_index("layer"), lax.axis_index("core")]).astype(jnp.int32)
    layers, n_core = lax.axis_size("layer"), lax.axis_size("core")
    n_z, n_hi, n_lo = lax.axis_size("z"), lax.axis_size("x_hi"), lax.axis_size("x_lo")
    rows, part = mlp_in.shape[1:]
    half, tokens = rows // 2, rows * n_lo * n_core
    gate, up, down = far(gate_weight[0].T), far(up_weight[0].T), far(down_weight[0])
    enc = pltpu.with_memory_space_constraint(enc_weight[0], pltpu.VMEM)
    dec = far(dec_weight[0])
    width, lat = enc.shape
    n_ff = gate.shape[0]
    dma = pltpu.SemaphoreType.DMA
    with jax.named_scope("gather_z"):
        block = jnp.concatenate([mlp_in[0, :half], mlp_in[0, half:]], axis=1)
        spread = jnp.broadcast_to(block, (n_z, half, 2 * part))
        spread, place = lax.optimization_barrier((spread, place))
        turned = [[turn(z, n_z) for z in range(n_z)]]
        got = lax.all_to_all(spread, "z", 0, 0, axis_index_groups=turned, tiled=True)
    with jax.named_scope("gather_x"):
        got = lax.all_to_all(jnp.broadcast_to(got, (n_hi * n_lo,) + got.shape), X, 0, 0, tiled=True)
    with jax.named_scope("gather_core"):
        got = lax.all_gather(got, "core", axis=0, tiled=False)
        got = got.reshape(n_core, n_hi, n_lo, n_z, half, 2 * part)
    with jax.named_scope("encode"):
        x, own, copies = call(
            encode_kernel,
            "encode",
            (
                jax.ShapeDtypeStruct((tokens, width), BF16),
                jax.ShapeDtypeStruct((tokens, lat), BF16),
                jax.ShapeDtypeStruct((layers, tokens, lat), BF16),
            ),
            [VMEM, VMEM, ANY],
            [pltpu.VMEM((1, lat), F32), dma((1,))],
            2 * tokens * width * lat,
            2 * width * lat,
            (VMEM, VMEM, VMEM),
        )(got, enc, far(enc_bias))
    with jax.named_scope("exchange"):
        every = lax.all_to_all(copies, "layer", 0, 0, tiled=True)
    with jax.named_scope("hidden"):
        partial, latent = call(
            hidden_kernel,
            "hidden",
            (jax.ShapeDtypeStruct((tokens, width), F32), jax.ShapeDtypeStruct((tokens, lat), BF16)),
            [SMEM, VMEM, VMEM] + [ANY] * 4,
            [pltpu.VMEM((n_ff, width), BF16) for _ in range(3)]
            + [pltpu.VMEM((lat, width), BF16), dma((4,))],
            6 * tokens * width * n_ff + 2 * tokens * width * lat,
            6 * n_ff * width + 2 * lat * width,
            (VMEM, VMEM),
        )(place, x, own, gate, up, down, dec)
    with jax.named_scope("decode"):
        half_sum = (tokens // n_core, width)
        keep, give = call(
            decode_kernel,
            "decode",
            (jax.ShapeDtypeStruct(half_sum, F32), jax.ShapeDtypeStruct(half_sum, BF16)),
            [SMEM, VMEM, VMEM, ANY],
            [
                pltpu.VMEM((tokens, width), F32),
                pltpu.VMEM((layers - 1, lat, width), BF16),
                dma((layers - 1,)),
            ],
            6 * tokens * width * lat,
            6 * lat * width,
            (VMEM, VMEM),
        )(place, every, partial, dec)
    with jax.named_scope("reduce_core"):
        got = lax.all_gather(give, "core", axis=0, tiled=False)
        send = call(
            join_kernel,
            "join",
            jax.ShapeDtypeStruct((n_hi, n_lo, n_z, half, 2 * part), BF16),
            [SMEM, VMEM, VMEM],
            [],
            0,
            8 * tokens * width,
        )(place, keep, got)
    with jax.named_scope("reduce_x"):
        got = lax.all_to_all(send.reshape(n_hi * n_lo, n_z, half, 2 * part), X, 0, 0, tiled=True)
        send = got.astype(F32).sum(0).astype(BF16)
    with jax.named_scope("reduce_z"):
        got = lax.all_to_all(send, "z", 0, 0, axis_index_groups=turned, tiled=True)
    with jax.named_scope("last"):
        error = call(
            last_kernel,
            "last",
            jax.ShapeDtypeStruct((rows, part), BF16),
            [VMEM],
            [],
            0,
            2 * n_z * rows * part,
        )(got)
    return error[None], latent[None]


def solution(mesh):
    return jax.shard_map(
        body,
        mesh=split_mesh(mesh),
        in_specs=(
            P("layer", DP, MP),
            P("layer", None, DP + MP),
            P("layer", None, DP + MP),
            P("layer", DP + MP, None),
            P("layer", None, DP + MP),
            P("layer", DP + MP),
            P("layer", None, DP + MP, None),
        ),
        out_specs=(P("layer", DP, MP), P("layer", None, DP + MP)),
        check_vma=False,
    )
```

```python
import jax
import jax.numpy as jnp
from jax import lax
from jax.experimental import pallas as pl
from jax.experimental.pallas import tpu as pltpu
from jax.sharding import Mesh, PartitionSpec as P

DP = ("x_lo", "core")
MP = ("z", "x_hi")
X = ("x_hi", "x_lo")
F32 = jnp.float32
BF16 = jnp.bfloat16
VMEM_BYTES = 8 * 2**20
VMEM = pl.BlockSpec(memory_space=pltpu.VMEM)
SMEM = pl.BlockSpec(memory_space=pltpu.SMEM)
ANY = pl.BlockSpec(memory_space=pl.ANY)


def split_mesh(mesh):
    return Mesh(mesh.devices.reshape(4, 2, 2, 16, 2), ("layer", "x_lo", "core", "z", "x_hi"))


def call(kernel, name, outs, specs, scratch, flops, n_bytes, out_specs=VMEM):
    return pl.pallas_call(
        kernel,
        name=name,
        out_shape=outs,
        in_specs=specs,
        out_specs=out_specs,
        scratch_shapes=scratch,
        cost_estimate=pl.CostEstimate(flops=flops, bytes_accessed=n_bytes, transcendentals=0),
        compiler_params=pltpu.CompilerParams(vmem_limit_bytes=VMEM_BYTES),
    )


def far(weight):
    return pltpu.with_memory_space_constraint(weight, pltpu.HBM)


def dot(a, b):
    return lax.dot_general(a, b, (((1,), (0,)), ((), ())), preferred_element_type=F32)


def dot_t(a, b):
    return lax.dot_general(a, b, (((1,), (1,)), ((), ())), preferred_element_type=F32)


def low_half(shape):
    return lax.broadcasted_iota(jnp.int32, shape, 1) < shape[1] // 2


def turn(z, n_z):
    return (z + n_z // 2) % n_z


def start_all(sems, pairs):
    copies = []
    for i, (source, target) in enumerate(pairs):
        copies.append(pltpu.make_async_copy(source, target, sems.at[i]))
        copies[-1].start()
    return copies


def wait_all(copies):
    for copy in copies:
        copy.wait()


def encode_kernel(got, enc, bias, x, own, copies, shift, sems):
    n_lo, n_core, n_z, n_hi, half, lanes = got.shape
    loads = start_all(sems, [(bias, shift)])
    low = low_half((half, lanes))
    for lo in range(n_lo):
        for core in range(n_core):
            row = (lo * n_core + core) * 2 * half
            for z in range(n_z):
                at = turn(z, n_z)
                a = got[lo, core, at, 0].astype(F32)
                b = got[lo, core, at, 1].astype(F32)
                top = jnp.where(low, a, pltpu.roll(b, lanes // 2, 1))
                bottom = jnp.where(low, pltpu.roll(a, lanes // 2, 1), b)
                cols = slice(z * lanes, (z + 1) * lanes)
                x[row : row + half, cols] = top.astype(BF16)
                x[row + half : row + 2 * half, cols] = bottom.astype(BF16)
    wait_all(loads)
    pre = dot(x[...], enc[...]) + shift[...]
    value = jnp.maximum(pre, F32(0.0)).astype(BF16)
    own[...] = value
    for s in range(copies.shape[0]):
        copies[s] = value


def hidden_kernel(place, x, own, gate, up, down, dec, out, latent, gates, ups, downs, decs, sems):
    loads = start_all(
        sems, [(gate, gates), (up, ups), (down, downs), (dec.at[place[0]], decs)]
    )
    latent[...] = own[...]
    rows = x[...]
    wait_all(loads[:2])
    gate_part = dot_t(rows, gates[...])
    up_part = dot_t(rows, ups[...])
    hidden = (gate_part / (1.0 + jnp.exp(-gate_part)) * up_part).astype(BF16)
    wait_all(loads[2:])
    tile = 256
    for n in range(0, x.shape[1], tile):
        cols = slice(n, n + tile)
        out[:, cols] = dot(hidden, downs[:, cols]) - dot(own[...], decs[:, cols])


def decode_kernel(place, got, partial, dec, keep, give, total, decs, sems):
    n_src = got.shape[0]
    layer, core = place[0], place[1]

    def load(back):
        return pltpu.make_async_copy(dec.at[layer - back], decs.at[back - 1], sems.at[back - 1])

    for back in range(1, n_src):

        @pl.when(layer >= back)
        def _():
            load(back).start()

    total[...] = partial[...]
    tile = 256
    for back in range(1, n_src):

        @pl.when(layer >= back)
        def _():
            load(back).wait()
            rows = got[layer - back]
            for n in range(0, total.shape[1], tile):
                total[:, n : n + tile] = total[:, n : n + tile] - dot(
                    rows, decs[back - 1, :, n : n + tile]
                )

    rows = keep.shape[0] // 2
    for lo in range(2):
        mine = pl.multiple_of((2 * lo + core) * rows, rows)
        theirs = pl.multiple_of((2 * lo + 1 - core) * rows, rows)
        keep[lo * rows : (lo + 1) * rows] = total[pl.ds(mine, rows)]
        give[lo * rows : (lo + 1) * rows] = total[pl.ds(theirs, rows)].astype(BF16)


def join_kernel(place, keep, got, out):
    n_hi, n_lo, n_z, half, lanes = out.shape
    other = 1 - place[1]
    low = low_half((half, lanes))
    for lo in range(n_lo):
        row = lo * 2 * half
        for z in range(n_z):
            cols = slice(z * lanes, (z + 1) * lanes)
            value = keep[row : row + 2 * half, cols] + got[other, row : row + 2 * half, cols].astype(F32)
            top, bottom = value[:half], value[half:]
            at = turn(z, n_z)
            out[0, lo, at] = jnp.where(low, top, pltpu.roll(bottom, lanes // 2, 1)).astype(BF16)
            out[1, lo, at] = jnp.where(low, pltpu.roll(top, lanes // 2, 1), bottom).astype(BF16)


def last_kernel(got, out):
    half, lanes = got.shape[1:]
    total = got[0].astype(F32)
    for z in range(1, got.shape[0]):
        total = total + got[z].astype(F32)
    out[0:half] = total[:, 0 : lanes // 2].astype(BF16)
    out[half : 2 * half] = pltpu.roll(total, lanes // 2, 1)[:, 0 : lanes // 2].astype(BF16)


def body(mlp_in, gate_weight, up_weight, down_weight, enc_weight, enc_bias, dec_weight):
    place = jnp.stack([lax.axis_index("layer"), lax.axis_index("core")]).astype(jnp.int32)
    layers, n_core = lax.axis_size("layer"), lax.axis_size("core")
    n_z, n_hi, n_lo = lax.axis_size("z"), lax.axis_size("x_hi"), lax.axis_size("x_lo")
    rows, part = mlp_in.shape[1:]
    half, tokens = rows // 2, rows * n_lo * n_core
    gate, up, down = far(gate_weight[0].T), far(up_weight[0].T), far(down_weight[0])
    enc = pltpu.with_memory_space_constraint(enc_weight[0], pltpu.VMEM)
    dec = far(dec_weight[0])
    width, lat = enc.shape
    n_ff = gate.shape[0]
    dma = pltpu.SemaphoreType.DMA
    turned = [[turn(z, n_z) for z in range(n_z)]]
    with jax.named_scope("gather_mp"):
        block = jnp.concatenate([mlp_in[0, :half], mlp_in[0, half:]], axis=1)
        spread = jnp.broadcast_to(block, (n_z * n_hi, half, 2 * part))
        spread, place = lax.optimization_barrier((spread, place))
        pairs = [[turn(z, n_z) * n_hi + hi for z in range(n_z) for hi in range(n_hi)]]
        got = lax.all_to_all(spread, MP, 0, 0, axis_index_groups=pairs, tiled=True)
    with jax.named_scope("gather_dp"):
        got = lax.all_gather(got, DP, axis=0, tiled=False)
        got = got.reshape(n_lo, n_core, n_z, n_hi, half, 2 * part)
    with jax.named_scope("encode"):
        x, own, copies = call(
            encode_kernel,
            "encode",
            (
                jax.ShapeDtypeStruct((tokens, width), BF16),
                jax.ShapeDtypeStruct((tokens, lat), BF16),
                jax.ShapeDtypeStruct((layers, tokens, lat), BF16),
            ),
            [VMEM, VMEM, ANY],
            [pltpu.VMEM((1, lat), F32), dma((1,))],
            2 * tokens * width * lat,
            2 * width * lat,
            (VMEM, VMEM, VMEM),
        )(got, enc, far(enc_bias))
    with jax.named_scope("exchange"):
        every = lax.all_to_all(copies, "layer", 0, 0, tiled=True)
    with jax.named_scope("hidden"):
        partial, latent = call(
            hidden_kernel,
            "hidden",
            (jax.ShapeDtypeStruct((tokens, width), F32), jax.ShapeDtypeStruct((tokens, lat), BF16)),
            [SMEM, VMEM, VMEM] + [ANY] * 4,
            [pltpu.VMEM((n_ff, width), BF16) for _ in range(3)]
            + [pltpu.VMEM((lat, width), BF16), dma((4,))],
            6 * tokens * width * n_ff + 2 * tokens * width * lat,
            6 * n_ff * width + 2 * lat * width,
            (VMEM, VMEM),
        )(place, x, own, gate, up, down, dec)
    with jax.named_scope("decode"):
        half_sum = (tokens // n_core, width)
        keep, give = call(
            decode_kernel,
            "decode",
            (jax.ShapeDtypeStruct(half_sum, F32), jax.ShapeDtypeStruct(half_sum, BF16)),
            [SMEM, VMEM, VMEM, ANY],
            [
                pltpu.VMEM((tokens, width), F32),
                pltpu.VMEM((layers - 1, lat, width), BF16),
                dma((layers - 1,)),
            ],
            6 * tokens * width * lat,
            6 * lat * width,
            (VMEM, VMEM),
        )(place, every, partial, dec)
    with jax.named_scope("reduce_core"):
        got = lax.all_gather(give, "core", axis=0, tiled=False)
        send = call(
            join_kernel,
            "join",
            jax.ShapeDtypeStruct((n_hi, n_lo, n_z, half, 2 * part), BF16),
            [SMEM, VMEM, VMEM],
            [],
            0,
            8 * tokens * width,
        )(place, keep, got)
    with jax.named_scope("reduce_x"):
        got = lax.all_to_all(send.reshape(n_hi * n_lo, n_z, half, 2 * part), X, 0, 0, tiled=True)
        send = got.astype(F32).sum(0).astype(BF16)
    with jax.named_scope("reduce_z"):
        got = lax.all_to_all(send, "z", 0, 0, axis_index_groups=turned, tiled=True)
    with jax.named_scope("last"):
        error = call(
            last_kernel,
            "last",
            jax.ShapeDtypeStruct((rows, part), BF16),
            [VMEM],
            [],
            0,
            2 * n_z * rows * part,
        )(got)
    return error[None], latent[None]


def solution(mesh):
    return jax.shard_map(
        body,
        mesh=split_mesh(mesh),
        in_specs=(
            P("layer", DP, MP),
            P("layer", None, DP + MP),
            P("layer", None, DP + MP),
            P("layer", DP + MP, None),
            P("layer", None, DP + MP),
            P("layer", DP + MP),
            P("layer", None, DP + MP, None),
        ),
        out_specs=(P("layer", DP, MP), P("layer", None, DP + MP)),
        check_vma=False,
    )
```

```python
import jax
import jax.numpy as jnp
from jax import lax
from jax.experimental import pallas as pl
from jax.experimental.pallas import tpu as pltpu
from jax.sharding import Mesh, PartitionSpec as P

DP = ("x_lo", "core")
MP = ("z", "x_hi")
X = ("x_hi", "x_lo")
F32 = jnp.float32
BF16 = jnp.bfloat16
VMEM_BYTES = 8 * 2**20
VMEM = pl.BlockSpec(memory_space=pltpu.VMEM)
ANY = pl.BlockSpec(memory_space=pl.ANY)


def split_mesh(mesh):
    return Mesh(mesh.devices.reshape(4, 2, 2, 16, 2), ("layer", "x_lo", "core", "z", "x_hi"))


def call(kernel, name, outs, specs, scratch, flops, n_bytes, out_specs=VMEM):
    return pl.pallas_call(
        kernel,
        name=name,
        out_shape=outs,
        in_specs=specs,
        out_specs=out_specs,
        scratch_shapes=scratch,
        cost_estimate=pl.CostEstimate(flops=flops, bytes_accessed=n_bytes, transcendentals=0),
        compiler_params=pltpu.CompilerParams(vmem_limit_bytes=VMEM_BYTES),
    )


def far(weight):
    return pltpu.with_memory_space_constraint(weight, pltpu.HBM)


def dot(a, b):
    return lax.dot_general(a, b, (((1,), (0,)), ((), ())), preferred_element_type=F32)


def dot_t(a, b):
    return lax.dot_general(a, b, (((1,), (1,)), ((), ())), preferred_element_type=F32)


def low_half(shape):
    return lax.broadcasted_iota(jnp.int32, shape, 1) < shape[1] // 2


def turn(z, n_z):
    return (z + n_z // 2) % n_z


def start_all(sems, pairs):
    copies = []
    for i, (source, target) in enumerate(pairs):
        copies.append(pltpu.make_async_copy(source, target, sems.at[i]))
        copies[-1].start()
    return copies


def wait_all(copies):
    for copy in copies:
        copy.wait()


def encode_kernel(got, enc, bias, x, own, copies, shift, sems):
    n_core, n_hi, n_lo, n_z, half, lanes = got.shape
    loads = start_all(sems, [(bias, shift)])
    low = low_half((half, lanes))
    for lo in range(n_lo):
        for core in range(n_core):
            row = (lo * n_core + core) * 2 * half
            for z in range(n_z):
                at = turn(z, n_z)
                a = got[core, 0, lo, at].astype(F32)
                b = got[core, 1, lo, at].astype(F32)
                top = jnp.where(low, a, pltpu.roll(b, lanes // 2, 1))
                bottom = jnp.where(low, pltpu.roll(a, lanes // 2, 1), b)
                cols = slice(z * lanes, (z + 1) * lanes)
                x[row : row + half, cols] = top.astype(BF16)
                x[row + half : row + 2 * half, cols] = bottom.astype(BF16)
    wait_all(loads)
    pre = dot(x[...], enc[...]) + shift[...]
    value = jnp.maximum(pre, F32(0.0)).astype(BF16)
    own[...] = value
    for s in range(copies.shape[0]):
        copies[s] = value


def hidden_kernel(x, own, gate, up, down, dec, out, latent, gates, ups, downs, decs, sems):
    loads = start_all(
        sems, [(gate, gates), (up, ups), (down, downs), (dec.at[lax.axis_index("layer")], decs)]
    )
    latent[...] = own[...]
    rows = x[...]
    wait_all(loads[:2])
    gate_part = dot_t(rows, gates[...])
    up_part = dot_t(rows, ups[...])
    hidden = (gate_part / (1.0 + jnp.exp(-gate_part)) * up_part).astype(BF16)
    wait_all(loads[2:])
    tile = 256
    for n in range(0, x.shape[1], tile):
        cols = slice(n, n + tile)
        out[:, cols] = dot(hidden, downs[:, cols]) - dot(own[...], decs[:, cols])


def decode_kernel(got, partial, dec, keep, give, total, decs, sems):
    n_src = got.shape[0]
    layer, core = lax.axis_index("layer"), lax.axis_index("core")

    def load(back):
        return pltpu.make_async_copy(dec.at[layer - back], decs.at[back - 1], sems.at[back - 1])

    for back in range(1, n_src):

        @pl.when(layer >= back)
        def _():
            load(back).start()

    total[...] = partial[...]
    tile = 256
    for back in range(1, n_src):

        @pl.when(layer >= back)
        def _():
            load(back).wait()
            rows = got[layer - back]
            for n in range(0, total.shape[1], tile):
                total[:, n : n + tile] = total[:, n : n + tile] - dot(
                    rows, decs[back - 1, :, n : n + tile]
                )

    rows = keep.shape[0] // 2
    for lo in range(2):
        mine = pl.multiple_of((2 * lo + core) * rows, rows)
        theirs = pl.multiple_of((2 * lo + 1 - core) * rows, rows)
        keep[lo * rows : (lo + 1) * rows] = total[pl.ds(mine, rows)]
        give[lo * rows : (lo + 1) * rows] = total[pl.ds(theirs, rows)].astype(BF16)


def join_kernel(keep, got, out):
    n_hi, n_lo, n_z, half, lanes = out.shape
    other = 1 - lax.axis_index("core")
    low = low_half((half, lanes))
    for lo in range(n_lo):
        row = lo * 2 * half
        for z in range(n_z):
            cols = slice(z * lanes, (z + 1) * lanes)
            value = keep[row : row + 2 * half, cols] + got[other, row : row + 2 * half, cols].astype(F32)
            top, bottom = value[:half], value[half:]
            at = turn(z, n_z)
            out[0, lo, at] = jnp.where(low, top, pltpu.roll(bottom, lanes // 2, 1)).astype(BF16)
            out[1, lo, at] = jnp.where(low, pltpu.roll(top, lanes // 2, 1), bottom).astype(BF16)


def last_kernel(got, out):
    half, lanes = got.shape[1:]
    total = got[0].astype(F32)
    for z in range(1, got.shape[0]):
        total = total + got[z].astype(F32)
    out[0:half] = total[:, 0 : lanes // 2].astype(BF16)
    out[half : 2 * half] = pltpu.roll(total, lanes // 2, 1)[:, 0 : lanes // 2].astype(BF16)


def body(mlp_in, gate_weight, up_weight, down_weight, enc_weight, enc_bias, dec_weight):
    layers, n_core = lax.axis_size("layer"), lax.axis_size("core")
    n_z, n_hi, n_lo = lax.axis_size("z"), lax.axis_size("x_hi"), lax.axis_size("x_lo")
    rows, part = mlp_in.shape[1:]
    half, tokens = rows // 2, rows * n_lo * n_core
    gate, up, down = far(gate_weight[0].T), far(up_weight[0].T), far(down_weight[0])
    enc = pltpu.with_memory_space_constraint(enc_weight[0], pltpu.VMEM)
    dec = far(dec_weight[0])
    width, lat = enc.shape
    n_ff = gate.shape[0]
    dma = pltpu.SemaphoreType.DMA
    with jax.named_scope("gather_z"):
        block = jnp.concatenate([mlp_in[0, :half], mlp_in[0, half:]], axis=1)
        spread = jnp.broadcast_to(block, (n_z, half, 2 * part))
        turned = [[turn(z, n_z) for z in range(n_z)]]
        got = lax.all_to_all(spread, "z", 0, 0, axis_index_groups=turned, tiled=True)
    with jax.named_scope("gather_x"):
        got = lax.all_to_all(jnp.broadcast_to(got, (n_hi * n_lo,) + got.shape), X, 0, 0, tiled=True)
    with jax.named_scope("gather_core"):
        got = lax.all_gather(got, "core", axis=0, tiled=False)
        got = got.reshape(n_core, n_hi, n_lo, n_z, half, 2 * part)
    with jax.named_scope("encode"):
        x, own, copies = call(
            encode_kernel,
            "encode",
            (
                jax.ShapeDtypeStruct((tokens, width), BF16),
                jax.ShapeDtypeStruct((tokens, lat), BF16),
                jax.ShapeDtypeStruct((layers, tokens, lat), BF16),
            ),
            [VMEM, VMEM, ANY],
            [pltpu.VMEM((1, lat), F32), dma((1,))],
            2 * tokens * width * lat,
            2 * width * lat,
            (VMEM, VMEM, VMEM),
        )(got, enc, far(enc_bias))
    with jax.named_scope("exchange"):
        every = lax.all_to_all(copies, "layer", 0, 0, tiled=True)
    with jax.named_scope("hidden"):
        partial, latent = call(
            hidden_kernel,
            "hidden",
            (jax.ShapeDtypeStruct((tokens, width), F32), jax.ShapeDtypeStruct((tokens, lat), BF16)),
            [VMEM, VMEM] + [ANY] * 4,
            [pltpu.VMEM((n_ff, width), BF16) for _ in range(3)]
            + [pltpu.VMEM((lat, width), BF16), dma((4,))],
            6 * tokens * width * n_ff + 2 * tokens * width * lat,
            6 * n_ff * width + 2 * lat * width,
            (VMEM, VMEM),
        )(x, own, gate, up, down, dec)
    with jax.named_scope("decode"):
        half_sum = (tokens // n_core, width)
        keep, give = call(
            decode_kernel,
            "decode",
            (jax.ShapeDtypeStruct(half_sum, F32), jax.ShapeDtypeStruct(half_sum, BF16)),
            [VMEM, VMEM, ANY],
            [
                pltpu.VMEM((tokens, width), F32),
                pltpu.VMEM((layers - 1, lat, width), BF16),
                dma((layers - 1,)),
            ],
            6 * tokens * width * lat,
            6 * lat * width,
            (VMEM, VMEM),
        )(every, partial, dec)
    with jax.named_scope("reduce_core"):
        got = lax.all_gather(give, "core", axis=0, tiled=False)
        send = call(
            join_kernel,
            "join",
            jax.ShapeDtypeStruct((n_hi, n_lo, n_z, half, 2 * part), BF16),
            [VMEM, VMEM],
            [],
            0,
            8 * tokens * width,
        )(keep, got)
    with jax.named_scope("reduce_x"):
        got = lax.all_to_all(send.reshape(n_hi * n_lo, n_z, half, 2 * part), X, 0, 0, tiled=True)
        send = got.astype(F32).sum(0).astype(BF16)
    with jax.named_scope("reduce_z"):
        got = lax.all_to_all(send, "z", 0, 0, axis_index_groups=turned, tiled=True)
    with jax.named_scope("last"):
        error = call(
            last_kernel,
            "last",
            jax.ShapeDtypeStruct((rows, part), BF16),
            [VMEM],
            [],
            0,
            2 * n_z * rows * part,
        )(got)
    return error[None], latent[None]


def solution(mesh):
    return jax.shard_map(
        body,
        mesh=split_mesh(mesh),
        in_specs=(
            P("layer", DP, MP),
            P("layer", None, DP + MP),
            P("layer", None, DP + MP),
            P("layer", DP + MP, None),
            P("layer", None, DP + MP),
            P("layer", DP + MP),
            P("layer", None, DP + MP, None),
        ),
        out_specs=(P("layer", DP, MP), P("layer", None, DP + MP)),
        check_vma=False,
    )
```

```python
import jax
import jax.numpy as jnp
from jax import lax
from jax.experimental import pallas as pl
from jax.experimental.pallas import tpu as pltpu
from jax.sharding import Mesh, PartitionSpec as P

DP = ("x_lo", "core")
MP = ("z", "x_hi")
X = ("core", "x_hi", "x_lo")
Z = ("core", "z")
F32 = jnp.float32
BF16 = jnp.bfloat16
VMEM_BYTES = 8 * 2**20
VMEM = pl.BlockSpec(memory_space=pltpu.VMEM)
ANY = pl.BlockSpec(memory_space=pl.ANY)


def split_mesh(mesh):
    return Mesh(mesh.devices.reshape(4, 2, 2, 16, 2), ("layer", "x_lo", "core", "z", "x_hi"))


def call(kernel, name, outs, specs, scratch, flops, n_bytes, out_specs=VMEM):
    return pl.pallas_call(
        kernel,
        name=name,
        out_shape=outs,
        in_specs=specs,
        out_specs=out_specs,
        scratch_shapes=scratch,
        cost_estimate=pl.CostEstimate(flops=flops, bytes_accessed=n_bytes, transcendentals=0),
        compiler_params=pltpu.CompilerParams(vmem_limit_bytes=VMEM_BYTES),
    )


def far(weight):
    return pltpu.with_memory_space_constraint(weight, pltpu.HBM)


def dot(a, b):
    return lax.dot_general(a, b, (((1,), (0,)), ((), ())), preferred_element_type=F32)


def dot_t(a, b):
    return lax.dot_general(a, b, (((1,), (1,)), ((), ())), preferred_element_type=F32)


def low_half(shape):
    return lax.broadcasted_iota(jnp.int32, shape, 1) < shape[1] // 2


def z_place(core, z, n_z):
    return (z + n_z // 2) % n_z if core == 0 else (n_z // 2 - z) % n_z


def x_place(core, x, n_x):
    return x if core == 0 else -x % n_x


def groups(place, n_core, n):
    found = []
    for core in range(n_core):
        order = sorted(range(n), key=lambda i: place(core, i, n))
        found.append([core * n + i for i in order])
    return found


def start_all(sems, pairs):
    copies = []
    for i, (source, target) in enumerate(pairs):
        copies.append(pltpu.make_async_copy(source, target, sems.at[i]))
        copies[-1].start()
    return copies


def wait_all(copies):
    for copy in copies:
        copy.wait()


def encode_kernel(got, enc, bias, x, own, copies, shift, sems):
    n_core, n_x, n_z, half, lanes = got.shape
    n_lo = 2
    loads = start_all(sems, [(bias, shift)])
    low = low_half((half, lanes))
    for lo in range(n_lo):
        for core in range(n_core):
            row = (lo * n_core + core) * 2 * half
            for z in range(n_z):
                at = z_place(core, z, n_z)
                a = got[core, x_place(core, lo, n_x), at].astype(F32)
                b = got[core, x_place(core, n_lo + lo, n_x), at].astype(F32)
                top = jnp.where(low, a, pltpu.roll(b, lanes // 2, 1))
                bottom = jnp.where(low, pltpu.roll(a, lanes // 2, 1), b)
                cols = slice(z * lanes, (z + 1) * lanes)
                x[row : row + half, cols] = top.astype(BF16)
                x[row + half : row + 2 * half, cols] = bottom.astype(BF16)
    pre = dot(x[...], enc[...])
    wait_all(loads)
    pre = pre + shift[...]
    value = jnp.maximum(pre, F32(0.0)).astype(BF16)
    own[...] = value
    for s in range(copies.shape[0]):
        copies[s] = value


def hidden_kernel(x, own, gate, up, down, dec, out, latent, gates, ups, downs, decs, sems):
    loads = start_all(
        sems, [(gate, gates), (up, ups), (down, downs), (dec.at[lax.axis_index("layer")], decs)]
    )
    latent[...] = own[...]
    rows = x[...]
    wait_all(loads[:2])
    gate_part = dot_t(rows, gates[...])
    up_part = dot_t(rows, ups[...])
    hidden = (gate_part / (1.0 + jnp.exp(-gate_part)) * up_part).astype(BF16)
    wait_all(loads[2:])
    tile = 256
    for n in range(0, x.shape[1], tile):
        cols = slice(n, n + tile)
        out[:, cols] = dot(hidden, downs[:, cols]) - dot(own[...], decs[:, cols])


def decode_kernel(got, partial, dec, keep, give, total, decs, sems):
    n_src = got.shape[0]
    layer, core = lax.axis_index("layer"), lax.axis_index("core")

    def load(back):
        return pltpu.make_async_copy(dec.at[layer - back], decs.at[back - 1], sems.at[back - 1])

    for back in range(1, n_src):

        @pl.when(layer >= back)
        def _():
            load(back).start()

    total[...] = partial[...]
    tile = 256
    for back in range(1, n_src):

        @pl.when(layer >= back)
        def _():
            load(back).wait()
            rows = got[layer - back]
            for n in range(0, total.shape[1], tile):
                total[:, n : n + tile] = total[:, n : n + tile] - dot(
                    rows, decs[back - 1, :, n : n + tile]
                )

    rows = keep.shape[0] // 2
    for lo in range(2):
        mine = pl.multiple_of((2 * lo + core) * rows, rows)
        theirs = pl.multiple_of((2 * lo + 1 - core) * rows, rows)
        keep[lo * rows : (lo + 1) * rows] = total[pl.ds(mine, rows)]
        give[lo * rows : (lo + 1) * rows] = total[pl.ds(theirs, rows)].astype(BF16)


def join_kernel(keep, got, out):
    n_x, n_z, half, lanes = out.shape
    n_lo = 2
    core = lax.axis_index("core")
    other = 1 - core
    low = low_half((half, lanes))

    def pick(place, i, n):
        return jnp.where(core == 0, place(0, i, n), place(1, i, n))

    for lo in range(n_lo):
        row = lo * 2 * half
        left, right = pick(x_place, lo, n_x), pick(x_place, n_lo + lo, n_x)
        for z in range(n_z):
            cols = slice(z * lanes, (z + 1) * lanes)
            value = keep[row : row + 2 * half, cols] + got[other, row : row + 2 * half, cols].astype(F32)
            top, bottom = value[:half], value[half:]
            at = pick(z_place, z, n_z)
            out[left, at] = jnp.where(low, top, pltpu.roll(bottom, lanes // 2, 1)).astype(BF16)
            out[right, at] = jnp.where(low, pltpu.roll(top, lanes // 2, 1), bottom).astype(BF16)


def last_kernel(got, out):
    half, lanes = got.shape[1:]
    total = got[0].astype(F32)
    for z in range(1, got.shape[0]):
        total = total + got[z].astype(F32)
    out[0:half] = total[:, 0 : lanes // 2].astype(BF16)
    out[half : 2 * half] = pltpu.roll(total, lanes // 2, 1)[:, 0 : lanes // 2].astype(BF16)


def body(mlp_in, gate_weight, up_weight, down_weight, enc_weight, enc_bias, dec_weight):
    layers, n_core = lax.axis_size("layer"), lax.axis_size("core")
    n_z, n_hi, n_lo = lax.axis_size("z"), lax.axis_size("x_hi"), lax.axis_size("x_lo")
    n_x = n_hi * n_lo
    z_groups, x_groups = groups(z_place, n_core, n_z), groups(x_place, n_core, n_x)
    rows, part = mlp_in.shape[1:]
    half, tokens = rows // 2, rows * n_lo * n_core
    gate, up, down = far(gate_weight[0].T), far(up_weight[0].T), far(down_weight[0])
    enc = pltpu.with_memory_space_constraint(enc_weight[0], pltpu.VMEM)
    dec = far(dec_weight[0])
    width, lat = enc.shape
    n_ff = gate.shape[0]
    dma = pltpu.SemaphoreType.DMA
    with jax.named_scope("gather_z"):
        block = jnp.concatenate([mlp_in[0, :half], mlp_in[0, half:]], axis=1)
        spread = jnp.broadcast_to(block, (n_z, half, 2 * part))
        got = lax.all_to_all(spread, Z, 0, 0, axis_index_groups=z_groups, tiled=True)
    with jax.named_scope("gather_x"):
        spread = jnp.broadcast_to(got[None], (n_x,) + got.shape)
        got = lax.all_to_all(spread, X, 0, 0, axis_index_groups=x_groups, tiled=True)
    with jax.named_scope("gather_core"):
        got = lax.all_gather(got, "core", axis=0, tiled=False)
    with jax.named_scope("encode"):
        x, own, copies = call(
            encode_kernel,
            "encode",
            (
                jax.ShapeDtypeStruct((tokens, width), BF16),
                jax.ShapeDtypeStruct((tokens, lat), BF16),
                jax.ShapeDtypeStruct((layers, tokens, lat), BF16),
            ),
            [VMEM, VMEM, ANY],
            [pltpu.VMEM((1, lat), F32), dma((1,))],
            2 * tokens * width * lat,
            2 * width * lat,
            (VMEM, VMEM, VMEM),
        )(got, enc, far(enc_bias))
    with jax.named_scope("exchange"):
        every = lax.all_to_all(copies, "layer", 0, 0, tiled=True)
    with jax.named_scope("hidden"):
        partial, latent = call(
            hidden_kernel,
            "hidden",
            (jax.ShapeDtypeStruct((tokens, width), F32), jax.ShapeDtypeStruct((tokens, lat), BF16)),
            [VMEM, VMEM] + [ANY] * 4,
            [pltpu.VMEM((n_ff, width), BF16) for _ in range(3)]
            + [pltpu.VMEM((lat, width), BF16), dma((4,))],
            6 * tokens * width * n_ff + 2 * tokens * width * lat,
            6 * n_ff * width + 2 * lat * width,
            (VMEM, VMEM),
        )(x, own, gate, up, down, dec)
    with jax.named_scope("decode"):
        half_sum = (tokens // n_core, width)
        keep, give = call(
            decode_kernel,
            "decode",
            (jax.ShapeDtypeStruct(half_sum, F32), jax.ShapeDtypeStruct(half_sum, BF16)),
            [VMEM, VMEM, ANY],
            [
                pltpu.VMEM((tokens, width), F32),
                pltpu.VMEM((layers - 1, lat, width), BF16),
                dma((layers - 1,)),
            ],
            6 * tokens * width * lat,
            6 * lat * width,
            (VMEM, VMEM),
        )(every, partial, dec)
    with jax.named_scope("reduce_core"):
        got = lax.all_gather(give, "core", axis=0, tiled=False)
        send = call(
            join_kernel,
            "join",
            jax.ShapeDtypeStruct((n_x, n_z, half, 2 * part), BF16),
            [VMEM, VMEM],
            [],
            0,
            8 * tokens * width,
        )(keep, got)
    with jax.named_scope("reduce_x"):
        got = lax.all_to_all(send, X, 0, 0, axis_index_groups=x_groups, tiled=True)
        send = got.astype(F32).sum(0).astype(BF16)
    with jax.named_scope("reduce_z"):
        got = lax.all_to_all(send, Z, 0, 0, axis_index_groups=z_groups, tiled=True)
    with jax.named_scope("last"):
        error = call(
            last_kernel,
            "last",
            jax.ShapeDtypeStruct((rows, part), BF16),
            [VMEM],
            [],
            0,
            2 * n_z * rows * part,
        )(got)
    return error[None], latent[None]


def solution(mesh):
    return jax.shard_map(
        body,
        mesh=split_mesh(mesh),
        in_specs=(
            P("layer", DP, MP),
            P("layer", None, DP + MP),
            P("layer", None, DP + MP),
            P("layer", DP + MP, None),
            P("layer", None, DP + MP),
            P("layer", DP + MP),
            P("layer", None, DP + MP, None),
        ),
        out_specs=(P("layer", DP, MP), P("layer", None, DP + MP)),
        check_vma=False,
    )
```

```python
import jax
import jax.numpy as jnp
from jax import lax
from jax.experimental import pallas as pl
from jax.experimental.pallas import tpu as pltpu
from jax.sharding import Mesh, PartitionSpec as P

DP = ("x_lo", "core")
MP = ("z", "x_hi")
X = ("x_hi", "x_lo")
F32 = jnp.float32
BF16 = jnp.bfloat16
VMEM_BYTES = 8 * 2**20
VMEM = pl.BlockSpec(memory_space=pltpu.VMEM)
ANY = pl.BlockSpec(memory_space=pl.ANY)


def split_mesh(mesh):
    return Mesh(mesh.devices.reshape(4, 2, 2, 16, 2), ("layer", "x_lo", "core", "z", "x_hi"))


def call(kernel, name, outs, specs, scratch, flops, n_bytes, out_specs=VMEM):
    return pl.pallas_call(
        kernel,
        name=name,
        out_shape=outs,
        in_specs=specs,
        out_specs=out_specs,
        scratch_shapes=scratch,
        cost_estimate=pl.CostEstimate(flops=flops, bytes_accessed=n_bytes, transcendentals=0),
        compiler_params=pltpu.CompilerParams(vmem_limit_bytes=VMEM_BYTES),
    )


def far(weight):
    return pltpu.with_memory_space_constraint(weight, pltpu.HBM)


def dot(a, b):
    return lax.dot_general(a, b, (((1,), (0,)), ((), ())), preferred_element_type=F32)


def dot_t(a, b):
    return lax.dot_general(a, b, (((1,), (1,)), ((), ())), preferred_element_type=F32)


def low_half(shape):
    return lax.broadcasted_iota(jnp.int32, shape, 1) < shape[1] // 2


def turn(z, n_z):
    return (z + n_z // 2) % n_z


def start_all(sems, pairs):
    copies = []
    for i, (source, target) in enumerate(pairs):
        copies.append(pltpu.make_async_copy(source, target, sems.at[i]))
        copies[-1].start()
    return copies


def wait_all(copies):
    for copy in copies:
        copy.wait()


def front_kernel(
    got, enc, dec, bias, gate, up, down, own, latent, out, x, shift, gates, ups, downs, decs, sems
):
    n_core, n_hi, n_lo, n_z, half, lanes = got.shape
    loads = start_all(
        sems,
        [(bias, shift), (gate, gates), (up, ups), (down, downs), (dec.at[lax.axis_index("layer")], decs)],
    )
    low = low_half((half, lanes))
    for lo in range(n_lo):
        for core in range(n_core):
            row = (lo * n_core + core) * 2 * half
            for z in range(n_z):
                at = turn(z, n_z)
                a = got[core, 0, lo, at].astype(F32)
                b = got[core, 1, lo, at].astype(F32)
                top = jnp.where(low, a, pltpu.roll(b, lanes // 2, 1))
                bottom = jnp.where(low, pltpu.roll(a, lanes // 2, 1), b)
                cols = slice(z * lanes, (z + 1) * lanes)
                x[row : row + half, cols] = top.astype(BF16)
                x[row + half : row + 2 * half, cols] = bottom.astype(BF16)
    rows = x[...]
    pre = dot(rows, enc[...])
    wait_all(loads)
    value = jnp.maximum(pre + shift[...], F32(0.0)).astype(BF16)
    own[...] = value
    latent[...] = value
    gate_part = dot_t(rows, gates[...])
    up_part = dot_t(rows, ups[...])
    hidden = (gate_part / (1.0 + jnp.exp(-gate_part)) * up_part).astype(BF16)
    tile = 256
    for n in range(0, x.shape[1], tile):
        cols = slice(n, n + tile)
        out[:, cols] = dot(hidden, downs[:, cols]) - dot(value, decs[:, cols])


def decode_kernel(got, partial, dec, keep, give, total):
    layer, core = lax.axis_index("layer"), lax.axis_index("core")
    total[...] = partial[...]
    tile = 256
    for back in range(1, got.shape[0]):

        @pl.when(layer >= back)
        def _():
            rows = got[layer - back]
            for n in range(0, total.shape[1], tile):
                cols = slice(n, n + tile)
                total[:, cols] = total[:, cols] - dot(rows, dec[layer - back, :, cols])

    rows = keep.shape[0] // 2
    for lo in range(2):
        mine = pl.multiple_of((2 * lo + core) * rows, rows)
        theirs = pl.multiple_of((2 * lo + 1 - core) * rows, rows)
        keep[lo * rows : (lo + 1) * rows] = total[pl.ds(mine, rows)]
        give[lo * rows : (lo + 1) * rows] = total[pl.ds(theirs, rows)].astype(BF16)


def join_kernel(keep, got, out):
    n_hi, n_lo, n_z, half, lanes = out.shape
    other = 1 - lax.axis_index("core")
    low = low_half((half, lanes))
    for lo in range(n_lo):
        row = lo * 2 * half
        for z in range(n_z):
            cols = slice(z * lanes, (z + 1) * lanes)
            value = keep[row : row + 2 * half, cols] + got[other, row : row + 2 * half, cols].astype(F32)
            top, bottom = value[:half], value[half:]
            at = turn(z, n_z)
            out[0, lo, at] = jnp.where(low, top, pltpu.roll(bottom, lanes // 2, 1)).astype(BF16)
            out[1, lo, at] = jnp.where(low, pltpu.roll(top, lanes // 2, 1), bottom).astype(BF16)


def last_kernel(got, out):
    half, lanes = got.shape[1:]
    total = got[0].astype(F32)
    for z in range(1, got.shape[0]):
        total = total + got[z].astype(F32)
    out[0:half] = total[:, 0 : lanes // 2].astype(BF16)
    out[half : 2 * half] = pltpu.roll(total, lanes // 2, 1)[:, 0 : lanes // 2].astype(BF16)


def body(mlp_in, gate_weight, up_weight, down_weight, enc_weight, enc_bias, dec_weight):
    layers, n_core = lax.axis_size("layer"), lax.axis_size("core")
    n_z, n_hi, n_lo = lax.axis_size("z"), lax.axis_size("x_hi"), lax.axis_size("x_lo")
    rows, part = mlp_in.shape[1:]
    half, tokens = rows // 2, rows * n_lo * n_core
    gate, up, down = far(gate_weight[0].T), far(up_weight[0].T), far(down_weight[0])
    enc = pltpu.with_memory_space_constraint(enc_weight[0], pltpu.VMEM)
    dec = pltpu.with_memory_space_constraint(dec_weight[0], pltpu.VMEM)
    width, lat = enc.shape
    n_ff = gate.shape[0]
    dma = pltpu.SemaphoreType.DMA
    with jax.named_scope("gather_z"):
        block = jnp.concatenate([mlp_in[0, :half], mlp_in[0, half:]], axis=1)
        spread = jnp.broadcast_to(block, (n_z, half, 2 * part))
        turned = [[turn(z, n_z) for z in range(n_z)]]
        got = lax.all_to_all(spread, "z", 0, 0, axis_index_groups=turned, tiled=True)
    with jax.named_scope("gather_x"):
        got = lax.all_to_all(jnp.broadcast_to(got, (n_hi * n_lo,) + got.shape), X, 0, 0, tiled=True)
    with jax.named_scope("gather_core"):
        got = lax.all_gather(got, "core", axis=0, tiled=False)
        got = got.reshape(n_core, n_hi, n_lo, n_z, half, 2 * part)
    with jax.named_scope("front"):
        own, latent, partial = call(
            front_kernel,
            "front",
            (
                jax.ShapeDtypeStruct((tokens, lat), BF16),
                jax.ShapeDtypeStruct((tokens, lat), BF16),
                jax.ShapeDtypeStruct((tokens, width), F32),
            ),
            [VMEM] * 2 + [ANY] * 5,
            [pltpu.VMEM((tokens, width), BF16), pltpu.VMEM((1, lat), F32)]
            + [pltpu.VMEM((n_ff, width), BF16) for _ in range(3)]
            + [pltpu.VMEM((lat, width), BF16), dma((5,))],
            6 * tokens * width * n_ff + 4 * tokens * width * lat,
            6 * n_ff * width + 4 * lat * width,
            (VMEM, VMEM, VMEM),
        )(got, enc, far(dec_weight[0]), far(enc_bias), gate, up, down)
    with jax.named_scope("exchange"):
        every = lax.all_gather(own, "layer", axis=0, tiled=False)
    with jax.named_scope("decode"):
        half_sum = (tokens // n_core, width)
        keep, give = call(
            decode_kernel,
            "decode",
            (jax.ShapeDtypeStruct(half_sum, F32), jax.ShapeDtypeStruct(half_sum, BF16)),
            [VMEM, VMEM, VMEM],
            [pltpu.VMEM((tokens, width), F32)],
            6 * tokens * width * lat,
            6 * lat * width,
            (VMEM, VMEM),
        )(every, partial, dec)
    with jax.named_scope("reduce_core"):
        got = lax.all_gather(give, "core", axis=0, tiled=False)
        send = call(
            join_kernel,
            "join",
            jax.ShapeDtypeStruct((n_hi, n_lo, n_z, half, 2 * part), BF16),
            [VMEM, VMEM],
            [],
            0,
            8 * tokens * width,
        )(keep, got)
    with jax.named_scope("reduce_x"):
        got = lax.all_to_all(send.reshape(n_hi * n_lo, n_z, half, 2 * part), X, 0, 0, tiled=True)
        send = got.astype(F32).sum(0).astype(BF16)
    with jax.named_scope("reduce_z"):
        got = lax.all_to_all(send, "z", 0, 0, axis_index_groups=turned, tiled=True)
    with jax.named_scope("last"):
        error = call(
            last_kernel,
            "last",
            jax.ShapeDtypeStruct((rows, part), BF16),
            [VMEM],
            [],
            0,
            2 * n_z * rows * part,
        )(got)
    return error[None], latent[None]


def solution(mesh):
    return jax.shard_map(
        body,
        mesh=split_mesh(mesh),
        in_specs=(
            P("layer", DP, MP),
            P("layer", None, DP + MP),
            P("layer", None, DP + MP),
            P("layer", DP + MP, None),
            P("layer", None, DP + MP),
            P("layer", DP + MP),
            P("layer", None, DP + MP, None),
        ),
        out_specs=(P("layer", DP, MP), P("layer", None, DP + MP)),
        check_vma=False,
    )
```

```python
import jax
import jax.numpy as jnp
from jax import lax
from jax.experimental import pallas as pl
from jax.experimental.pallas import tpu as pltpu
from jax.sharding import Mesh, PartitionSpec as P

DP = ("x_lo", "core")
MP = ("z", "x_hi")
X = ("x_hi", "x_lo")
F32 = jnp.float32
BF16 = jnp.bfloat16
VMEM_BYTES = 8 * 2**20
VMEM = pl.BlockSpec(memory_space=pltpu.VMEM)
ANY = pl.BlockSpec(memory_space=pl.ANY)


def split_mesh(mesh):
    return Mesh(mesh.devices.reshape(4, 2, 2, 16, 2), ("layer", "x_lo", "core", "z", "x_hi"))


def call(kernel, name, outs, specs, scratch, flops, n_bytes, out_specs=VMEM):
    return pl.pallas_call(
        kernel,
        name=name,
        out_shape=outs,
        in_specs=specs,
        out_specs=out_specs,
        scratch_shapes=scratch,
        cost_estimate=pl.CostEstimate(flops=flops, bytes_accessed=n_bytes, transcendentals=0),
        compiler_params=pltpu.CompilerParams(vmem_limit_bytes=VMEM_BYTES),
    )


def far(weight):
    return pltpu.with_memory_space_constraint(weight, pltpu.HBM)


def dot(a, b):
    return lax.dot_general(a, b, (((1,), (0,)), ((), ())), preferred_element_type=F32)


def dot_t(a, b):
    return lax.dot_general(a, b, (((1,), (1,)), ((), ())), preferred_element_type=F32)


def low_half(shape):
    return lax.broadcasted_iota(jnp.int32, shape, 1) < shape[1] // 2


def turn(z, n_z):
    return (z + n_z // 2) % n_z


def start_all(sems, pairs):
    copies = []
    for i, (source, target) in enumerate(pairs):
        copies.append(pltpu.make_async_copy(source, target, sems.at[i]))
        copies[-1].start()
    return copies


def wait_all(copies):
    for copy in copies:
        copy.wait()


def encode_kernel(got, enc, bias, x, own, copies, shift, sems):
    n_core, n_hi, n_lo, n_z, half, lanes = got.shape
    loads = start_all(sems, [(bias, shift)])
    low = low_half((half, lanes))
    for lo in range(n_lo):
        for core in range(n_core):
            row = (lo * n_core + core) * 2 * half
            for z in range(n_z):
                at = turn(z, n_z)
                a = got[core, 0, lo, at].astype(F32)
                b = got[core, 1, lo, at].astype(F32)
                top = jnp.where(low, a, pltpu.roll(b, lanes // 2, 1))
                bottom = jnp.where(low, pltpu.roll(a, lanes // 2, 1), b)
                cols = slice(z * lanes, (z + 1) * lanes)
                x[row : row + half, cols] = top.astype(BF16)
                x[row + half : row + 2 * half, cols] = bottom.astype(BF16)
    wait_all(loads)
    pre = dot(x[...], enc[...]) + shift[...]
    value = jnp.maximum(pre, F32(0.0)).astype(BF16)
    own[...] = value
    for s in range(copies.shape[0]):
        copies[s] = value


def hidden_kernel(x, own, gate, up, down, dec, out, latent, gates, ups, downs, decs, sems):
    loads = start_all(
        sems, [(gate, gates), (up, ups), (down, downs), (dec.at[lax.axis_index("layer")], decs)]
    )
    latent[...] = own[...]
    rows = x[...]
    wait_all(loads[:2])
    gate_part = dot_t(rows, gates[...])
    up_part = dot_t(rows, ups[...])
    hidden = (gate_part / (1.0 + jnp.exp(-gate_part)) * up_part).astype(BF16)
    wait_all(loads[2:])
    tile = 256
    for n in range(0, x.shape[1], tile):
        cols = slice(n, n + tile)
        out[:, cols] = dot(hidden, downs[:, cols]) - dot(own[...], decs[:, cols])


def decode_kernel(got, partial, dec, keep, give, total):
    layer, core = lax.axis_index("layer"), lax.axis_index("core")
    total[...] = partial[...]
    tile = 256
    for back in range(1, got.shape[0]):

        @pl.when(layer >= back)
        def _():
            rows = got[layer - back]
            for n in range(0, total.shape[1], tile):
                cols = slice(n, n + tile)
                total[:, cols] = total[:, cols] - dot(rows, dec[layer - back, :, cols])

    rows = keep.shape[0] // 2
    for lo in range(2):
        mine = pl.multiple_of((2 * lo + core) * rows, rows)
        theirs = pl.multiple_of((2 * lo + 1 - core) * rows, rows)
        keep[lo * rows : (lo + 1) * rows] = total[pl.ds(mine, rows)]
        give[lo * rows : (lo + 1) * rows] = total[pl.ds(theirs, rows)].astype(BF16)


def join_kernel(keep, got, out):
    n_hi, n_lo, n_z, half, lanes = out.shape
    other = 1 - lax.axis_index("core")
    low = low_half((half, lanes))
    for lo in range(n_lo):
        row = lo * 2 * half
        for z in range(n_z):
            cols = slice(z * lanes, (z + 1) * lanes)
            value = keep[row : row + 2 * half, cols] + got[other, row : row + 2 * half, cols].astype(F32)
            top, bottom = value[:half], value[half:]
            at = turn(z, n_z)
            out[0, lo, at] = jnp.where(low, top, pltpu.roll(bottom, lanes // 2, 1)).astype(BF16)
            out[1, lo, at] = jnp.where(low, pltpu.roll(top, lanes // 2, 1), bottom).astype(BF16)


def last_kernel(got, out):
    half, lanes = got.shape[1:]
    total = got[0].astype(F32)
    for z in range(1, got.shape[0]):
        total = total + got[z].astype(F32)
    out[0:half] = total[:, 0 : lanes // 2].astype(BF16)
    out[half : 2 * half] = pltpu.roll(total, lanes // 2, 1)[:, 0 : lanes // 2].astype(BF16)


def body(mlp_in, gate_weight, up_weight, down_weight, enc_weight, enc_bias, dec_weight):
    layers, n_core = lax.axis_size("layer"), lax.axis_size("core")
    n_z, n_hi, n_lo = lax.axis_size("z"), lax.axis_size("x_hi"), lax.axis_size("x_lo")
    rows, part = mlp_in.shape[1:]
    half, tokens = rows // 2, rows * n_lo * n_core
    gate, up, down = far(gate_weight[0].T), far(up_weight[0].T), far(down_weight[0])
    enc = pltpu.with_memory_space_constraint(enc_weight[0], pltpu.VMEM)
    dec = far(dec_weight[0])
    width, lat = enc.shape
    n_ff = gate.shape[0]
    dma = pltpu.SemaphoreType.DMA
    with jax.named_scope("gather_z"):
        block = jnp.concatenate([mlp_in[0, :half], mlp_in[0, half:]], axis=1)
        spread = jnp.broadcast_to(block, (n_z, half, 2 * part))
        turned = [[turn(z, n_z) for z in range(n_z)]]
        got = lax.all_to_all(spread, "z", 0, 0, axis_index_groups=turned, tiled=True)
    with jax.named_scope("gather_x"):
        got = lax.all_to_all(jnp.broadcast_to(got, (n_hi * n_lo,) + got.shape), X, 0, 0, tiled=True)
    with jax.named_scope("gather_core"):
        got = lax.all_gather(got, "core", axis=0, tiled=False)
        got = got.reshape(n_core, n_hi, n_lo, n_z, half, 2 * part)
    with jax.named_scope("encode"):
        x, own, copies = call(
            encode_kernel,
            "encode",
            (
                jax.ShapeDtypeStruct((tokens, width), BF16),
                jax.ShapeDtypeStruct((tokens, lat), BF16),
                jax.ShapeDtypeStruct((layers, tokens, lat), BF16),
            ),
            [VMEM, VMEM, ANY],
            [pltpu.VMEM((1, lat), F32), dma((1,))],
            2 * tokens * width * lat,
            2 * width * lat,
            (VMEM, VMEM, VMEM),
        )(got, enc, far(enc_bias))
    with jax.named_scope("exchange"):
        every = lax.all_to_all(copies, "layer", 0, 0, tiled=True)
    with jax.named_scope("hidden"):
        partial, latent = call(
            hidden_kernel,
            "hidden",
            (jax.ShapeDtypeStruct((tokens, width), F32), jax.ShapeDtypeStruct((tokens, lat), BF16)),
            [VMEM, VMEM] + [ANY] * 4,
            [pltpu.VMEM((n_ff, width), BF16) for _ in range(3)]
            + [pltpu.VMEM((lat, width), BF16), dma((4,))],
            6 * tokens * width * n_ff + 2 * tokens * width * lat,
            6 * n_ff * width + 2 * lat * width,
            (VMEM, VMEM),
        )(x, own, gate, up, down, dec)
    with jax.named_scope("decode"):
        half_sum = (tokens // n_core, width)
        keep, give = call(
            decode_kernel,
            "decode",
            (jax.ShapeDtypeStruct(half_sum, F32), jax.ShapeDtypeStruct(half_sum, BF16)),
            [VMEM, VMEM, VMEM],
            [pltpu.VMEM((tokens, width), F32)],
            6 * tokens * width * lat,
            6 * lat * width,
            (VMEM, VMEM),
        )(every, partial, pltpu.with_memory_space_constraint(dec_weight[0, : layers - 1], pltpu.VMEM))
    with jax.named_scope("reduce_core"):
        got = lax.all_gather(give, "core", axis=0, tiled=False)
        send = call(
            join_kernel,
            "join",
            jax.ShapeDtypeStruct((n_hi, n_lo, n_z, half, 2 * part), BF16),
            [VMEM, VMEM],
            [],
            0,
            8 * tokens * width,
        )(keep, got)
    with jax.named_scope("reduce_x"):
        got = lax.all_to_all(send.reshape(n_hi * n_lo, n_z, half, 2 * part), X, 0, 0, tiled=True)
        send = got.astype(F32).sum(0).astype(BF16)
    with jax.named_scope("reduce_z"):
        got = lax.all_to_all(send, "z", 0, 0, axis_index_groups=turned, tiled=True)
    with jax.named_scope("last"):
        error = call(
            last_kernel,
            "last",
            jax.ShapeDtypeStruct((rows, part), BF16),
            [VMEM],
            [],
            0,
            2 * n_z * rows * part,
        )(got)
    return error[None], latent[None]


def solution(mesh):
    return jax.shard_map(
        body,
        mesh=split_mesh(mesh),
        in_specs=(
            P("layer", DP, MP),
            P("layer", None, DP + MP),
            P("layer", None, DP + MP),
            P("layer", DP + MP, None),
            P("layer", None, DP + MP),
            P("layer", DP + MP),
            P("layer", None, DP + MP, None),
        ),
        out_specs=(P("layer", DP, MP), P("layer", None, DP + MP)),
        check_vma=False,
    )
```
